32 devices in a mesh: grp: 2 (over y), seq: 4 (over z), tp: 2 (over x), pr: 2 (over core).
Axes of the slice: x: 2, y: 2, z: 4, core: 2. Of those that a mesh axis runs over, the one named last changes fastest.
Arguments:
- dna_feats: bfloat16 [2048, 768], P(('grp', 'seq', 'pr'), 'tp'), parts along dimension 0, may hold values from -6 to 6
- conv_w: bfloat16 [5, 768, 1536], P(None, 'pr', 'tp'), may hold values from -0.09375 to 0.09375
- conv_gain: float32 [1536], P('tp'), may hold values from 0.1 to 1.9
- attn_gain: float32 [1536], replicated, may hold values from 0.1 to 1.9
- wq: bfloat16 [1536, 1024], P('pr', 'tp'), as said below
- wk: bfloat16 [1536, 1024], P('pr', 'tp'), as said below
- wv: bfloat16 [1536, 1536], P('pr', 'tp'), may hold values from -0.3125 to 0.3125
- wo: bfloat16 [1536, 1536], P('tp', 'pr'), may hold values from -0.15625 to 0.15625
- pair_w: bfloat16 [1536, 256], P('tp'), may hold values from -0.3125 to 0.3125
- pair_in: bfloat16 [128, 64, 128], P(('grp', 'seq', 'tp'), 'pr'), parts along dimension 0, may hold values from -6 to 6
- pair_gain: float32 [128], replicated, may hold values from 0.1 to 1.9
- pair_w1: bfloat16 [128, 256], replicated, may hold values from -0.5 to 0.5
- pair_w2: bfloat16 [256, 128], replicated, may hold values from -0.375 to 0.375
Outputs:
- trunk: bfloat16 [2048, 1536], P(('grp', 'seq', 'pr'), 'tp'), parts along dimension 0
- pair_out: bfloat16 [128, 64, 128], P(('grp', 'seq', 'tp'), 'pr'), parts along dimension 0
The draws below stay inside these ranges and needn't reach their ends.
There are 2 independent parts, one for each index of `grp`. The reference program is written for one: setup_inputs(seed, part) draws one part's arguments, and reference() takes and returns one part's arrays. A program takes and returns all parts, laid end to end along the dimension named above; an argument that names none is the same for every part. Nothing has to cross between parts.
Inputs may be any that keep to these rules, and one draw needn't show every extreme that they name: `wq`: before rounding to bfloat16, entries lie between -3.5 / sqrt(1536) and 3.5 / sqrt(1536). `wk`: before rounding to bfloat16, entries lie between -8.75 / sqrt(1536) and 8.75 / sqrt(1536).
All inputs are finite; a program needn't handle non-finite values.
Results may differ from the reference program's by a relative error of at most 0.013.
The reference program's roundings to bfloat16 on the way (of `hidden_conv`, `normed`, `weights`, `attended`, `embedded`, `pair_normed` and `inner`) count: a program that leaves them out, or rounds other values in their place, can miss the bound.
Values may be sent and summed in bfloat16 or wider, within the bound.
A program may use at most 64 MiB of HBM per device.

```python
import math
import jax
import jax.numpy as jnp
from jax import lax

KW = 5
C0 = 768
D = 1536
HEADS = 8
QK = 128
HV = 192
POOL = 16
PW = 128
PH = 256
L = 1024
P_SIZE = 64


def clipped_normal(key, salt):
    normal_draw = jax.random.normal(jax.random.fold_in(key, salt), (D, HEADS * QK), jnp.float32)
    return jnp.clip(normal_draw, -3.5, 3.5) / math.sqrt(D)


def draw_wq(key, part):
    base = clipped_normal(key, 101)
    result = base
    return result.astype(jnp.bfloat16)


def draw_wk(key, part):
    base = clipped_normal(key, 202)
    result = 2.5 * base
    return result.astype(jnp.bfloat16)


def levels(own_key, extent, shards, least, high):
    gain = 1.0
    for position, blocks in shards:
        steps = jax.random.uniform(jax.random.fold_in(jax.random.fold_in(own_key, 6), position), (blocks,), jnp.float32, least / len(shards), high / len(shards))
        gain = gain * jnp.repeat(jnp.exp(steps), extent[position] // blocks).reshape((-1,) + (1,) * (len(extent) - 1 - position))
    return gain


def scatter_about(rng, shape, scale, limit, split=(), dtype=jnp.bfloat16):
    entries = jax.random.normal(rng, shape, jnp.float32) * scale
    if len(split) > 0:
        entries = levels(rng, shape, split, -0.22, 0.18) * entries
    return jnp.clip(entries, min=-limit, max=limit).astype(dtype)


def setup_inputs(seed: int = 0, part: int = 0) -> dict:
    splits = jax.random.split(jax.random.key(seed), 14)
    own_keys = jax.random.split(jax.random.fold_in(splits[13], part), 14)
    return {
        "dna_feats": scatter_about(own_keys[0], (L, C0), 1.0, 6.0, ((0, 8), (1, 2))),
        "conv_w": scatter_about(splits[1], (KW, C0, D), (KW * C0) ** -0.5, 0.09375, ((1, 2), (2, 2))),
        "conv_gain": jnp.clip(1.0 + 0.18 * jax.random.normal(splits[2], (D,), jnp.float32), 0.1, 1.9),
        "attn_gain": jnp.clip(1.0 + 0.18 * jax.random.normal(splits[3], (D,), jnp.float32), 0.1, 1.9),
        "wq": draw_wq(jax.random.fold_in(splits[13], 71), part),
        "wk": draw_wk(jax.random.fold_in(splits[13], 71), part),
        "wv": scatter_about(splits[6], (D, HEADS * HV), (D // 4) ** -0.5, 0.3125, ((0, 2), (1, 2))),
        "wo": scatter_about(splits[7], (HEADS * HV, D), (HEADS * HV) ** -0.5, 0.15625, ((0, 2), (1, 2))),
        "pair_w": scatter_about(splits[8], (D, 2 * PW), (D // 4) ** -0.5, 0.3125, ((0, 2),)),
        "pair_in": scatter_about(own_keys[9], (P_SIZE, P_SIZE, PW), 1.0, 6.0, ((0, 8), (1, 2))),
        "pair_gain": jnp.clip(1.0 + 0.18 * jax.random.normal(splits[10], (PW,), jnp.float32), 0.1, 1.9),
        "pair_w1": scatter_about(splits[11], (PW, PH), PW ** -0.5, 0.5),
        "pair_w2": scatter_about(splits[12], (PH, PW), PH ** -0.5, 0.375),
    }


EPSILON = 1e-06

def rms_scale(values):
    return lax.rsqrt(lax.optimization_barrier(jnp.mean(values * values, axis=-1, keepdims=True)) + EPSILON)

def reference(dna_feats, conv_w, conv_gain, attn_gain, wq, wk, wv, wo, pair_w, pair_in, pair_gain, pair_w1, pair_w2):
    length = dna_feats.shape[0]
    reach = KW // 2
    padded = jnp.pad(dna_feats, ((reach, reach), (0, 0)))
    conv_out = jnp.zeros((length, conv_w.shape[2]), jnp.float32)
    for offset in range(KW):
        conv_out = conv_out + jnp.dot(padded[offset:offset + length], conv_w[offset], preferred_element_type=jnp.float32)
    hidden_conv = jax.nn.gelu(conv_out * rms_scale(conv_out) * conv_gain).astype(jnp.bfloat16)
    trunk_in = hidden_conv.astype(jnp.float32)
    normed = (trunk_in * rms_scale(trunk_in) * attn_gain).astype(jnp.bfloat16)
    queries = jnp.dot(normed, wq, preferred_element_type=jnp.float32).astype(jnp.bfloat16).reshape(length, HEADS, QK)
    keys_all = jnp.dot(normed, wk, preferred_element_type=jnp.float32).astype(jnp.bfloat16).reshape(length, HEADS, QK)
    values_all = jnp.dot(normed, wv, preferred_element_type=jnp.float32).astype(jnp.bfloat16).reshape(length, HEADS, HV)
    keys_wide = keys_all.astype(jnp.float32)
    values_wide = values_all.astype(jnp.float32)
    block = math.gcd(length, 512)
    factor = 1.0 / math.sqrt(QK)

    def attend_block(query_block):
        scores = jnp.einsum('qhd,khd->hqk', query_block.astype(jnp.float32), keys_wide) * factor
        highest = lax.optimization_barrier(jnp.max(scores, axis=-1, keepdims=True))
        weights = jnp.exp(scores - highest)
        totals = lax.optimization_barrier(jnp.sum(weights, axis=-1, keepdims=True))
        rounded = lax.optimization_barrier(weights.astype(jnp.bfloat16)).astype(jnp.float32)
        mixed = jnp.einsum('hqk,khd->qhd', rounded, values_wide)
        return mixed / jnp.transpose(totals, (1, 0, 2))
    attended = lax.map(attend_block, queries.reshape(length // block, block, HEADS, QK))
    attended = attended.reshape(length, HEADS * HV).astype(jnp.bfloat16)
    projected = jnp.dot(attended, wo, preferred_element_type=jnp.float32)
    trunk = (trunk_in + projected).astype(jnp.bfloat16)
    pooled = trunk.astype(jnp.float32).reshape(length // POOL, POOL, -1).mean(axis=1)
    embedded = jnp.dot(pooled, pair_w.astype(jnp.float32), precision=lax.Precision.HIGHEST).astype(jnp.bfloat16)
    row_part = embedded[:, :PW].astype(jnp.float32)
    column_part = embedded[:, PW:].astype(jnp.float32)
    summed = pair_in.astype(jnp.float32) + row_part[:, None, :] + column_part[None, :, :]
    pair_normed = (summed * rms_scale(summed) * pair_gain).astype(jnp.bfloat16)
    inner = jax.nn.gelu(jnp.dot(pair_normed.reshape(-1, PW), pair_w1, preferred_element_type=jnp.float32)).astype(jnp.bfloat16)
    update = jnp.dot(inner, pair_w2, preferred_element_type=jnp.float32).reshape(summed.shape)
    pair_out = (summed + update).astype(jnp.bfloat16)
    return (trunk, pair_out)
```

```python
import math

import jax
import jax.numpy as jnp
from jax import lax
from jax.experimental import pallas as pl
from jax.experimental.pallas import tpu as pltpu
from jax.sharding import PartitionSpec as P

QK = 128
HV = 192
POOL = 16


EPSILON = 1e-06


def extended(value, sides, width):
    for axis, dim in sides:
        devices, length = (lax.axis_size(axis), value.shape[dim])
        up = [(i, (i + 1) % devices) for i in range(devices - 1)]
        down = [(j, i) for i, j in up]
        last = lax.slice_in_dim(value, length - width, length, axis=dim)
        first = lax.slice_in_dim(value, 0, width, axis=dim)
        before = lax.ppermute(last, axis, up)
        after = lax.ppermute(first, axis, down)
        value = jnp.concatenate([before, value, after], axis=dim)
    return value


def rms_scale(values):
    return lax.rsqrt(jnp.mean(values * values, axis=-1, keepdims=True) + EPSILON)


def attention_start(query_block):
    head_count = query_block.shape[1]
    row_count = query_block.shape[0]
    highest = jnp.full((head_count, row_count), -1e30, jnp.float32)
    totals = jnp.zeros((head_count, row_count), jnp.float32)
    mixed = jnp.zeros((row_count, head_count, HV), jnp.float32)
    return (highest, totals, mixed)


def attention_step(query_block, carry, pieces):
    factor = 1.0 / math.sqrt(QK)
    highest, totals, mixed = carry
    key_piece, value_piece = pieces
    scores = (
        jnp.einsum("qhd,khd->hqk", query_block, key_piece, preferred_element_type=jnp.float32)
        * factor
    )
    new_high = jnp.maximum(highest, jnp.max(scores, axis=-1))
    weights = jnp.exp(scores - new_high[:, :, None])
    totals = jnp.sum(weights, axis=-1)
    added = jnp.einsum(
        "hqk,khd->qhd",
        weights.astype(jnp.bfloat16),
        value_piece,
        preferred_element_type=jnp.float32,
    )
    mixed = added
    return (new_high, totals, mixed)


def attention_finish(carry):
    highest, totals, mixed = carry
    return (mixed / jnp.transpose(totals)[:, :, None]).astype(jnp.bfloat16)


def local(
    dna_feats,
    conv_w,
    conv_gain,
    attn_gain,
    wq,
    wk,
    wv,
    wo,
    pair_w,
    pair_in,
    pair_gain,
    pair_w1,
    pair_w2,
):
    row_count = dna_feats.shape[0]
    reach = conv_w.shape[0] // 2
    rimmed = extended(dna_feats, ((("seq", "pr"), 0),), reach)
    channels = lax.all_gather(rimmed, "tp", axis=1, tiled=True)
    conv_empty = jnp.zeros((row_count, conv_w.shape[2]), jnp.float32)
    total = conv_empty
    piece = lax.all_gather(conv_w, "pr", axis=1, tiled=True)
    sliced = channels
    for offset in range(piece.shape[0]):
        total = total + jnp.dot(
            sliced[offset : offset + row_count], piece[offset], preferred_element_type=jnp.float32
        )
    squares = lax.psum(jnp.sum(total * total, axis=1, keepdims=True), "tp")
    model_width = total.shape[1] * lax.axis_size("tp")
    hidden_conv = jax.nn.gelu(
        total * lax.rsqrt(squares / model_width + EPSILON) * conv_gain
    ).astype(jnp.bfloat16)
    trunk_full = lax.all_gather(hidden_conv, "tp", axis=1, tiled=True)
    trunk_wide = trunk_full.astype(jnp.float32)
    normed = (trunk_wide * rms_scale(trunk_wide) * attn_gain).astype(jnp.bfloat16)
    query_width = wq.shape[1]
    pieces = (
        lax.all_gather(wq, "pr", axis=0, tiled=True),
        lax.all_gather(wk, "pr", axis=0, tiled=True),
        lax.all_gather(wv, "pr", axis=0, tiled=True),
    )
    sliced = normed
    query_sum, key_sum, value_sum = tuple(
        (jnp.dot(sliced, piece, preferred_element_type=jnp.float32) for piece in pieces)
    )
    head_count = query_width // QK
    queries = query_sum.astype(jnp.bfloat16).reshape(row_count, head_count, QK)
    keys_local = key_sum.astype(jnp.bfloat16).reshape(row_count, head_count, QK)
    values_local = value_sum.astype(jnp.bfloat16).reshape(row_count, head_count, HV)
    moved_query, moved_keys, moved_values = (
        lax.all_to_all(queries, "pr", split_axis=1, concat_axis=0, tiled=True),
        lax.all_to_all(keys_local, "pr", split_axis=1, concat_axis=0, tiled=True),
        lax.all_to_all(values_local, "pr", split_axis=1, concat_axis=0, tiled=True),
    )
    carried = attention_step(
        moved_query,
        attention_start(moved_query),
        (
            lax.all_gather(moved_keys, "seq", axis=0, tiled=True),
            lax.all_gather(moved_values, "seq", axis=0, tiled=True),
        ),
    )
    attended = lax.all_to_all(
        attention_finish(carried), "pr", split_axis=0, concat_axis=1, tiled=True
    )
    attended_flat = attended.reshape(row_count, head_count * HV)
    head_terms = jnp.dot(
        attended_flat,
        lax.all_gather(wo, "pr", axis=1, tiled=True),
        preferred_element_type=jnp.float32,
    )
    own_share = lax.psum_scatter(
        head_terms.astype(jnp.bfloat16), "tp", scatter_dimension=1, tiled=True
    ).astype(jnp.float32)
    trunk = (hidden_conv.astype(jnp.float32) + own_share).astype(jnp.bfloat16)
    pooled = trunk.astype(jnp.float32).reshape(row_count // POOL, POOL, -1).mean(axis=1)
    partial_embed = jnp.dot(pooled, pair_w.astype(jnp.float32), precision=lax.Precision.HIGHEST)
    embedded = lax.psum(partial_embed, "tp").astype(jnp.bfloat16)
    every_embed = lax.all_gather(embedded, ("seq", "pr"), axis=0, tiled=True)
    pair_rows = pair_in.shape[0]
    pair_cols = pair_in.shape[1]
    pair_width = pair_in.shape[2]
    row_first = lax.axis_index(("seq", "tp")) * pair_rows
    col_first = lax.axis_index("pr") * pair_cols
    row_embed = lax.dynamic_slice_in_dim(every_embed, row_first, pair_rows, 0)[
        :, :pair_width
    ].astype(jnp.float32)
    col_embed = lax.dynamic_slice_in_dim(every_embed, col_first, pair_cols, 0)[
        :, pair_width:
    ].astype(jnp.float32)
    summed = pair_in.astype(jnp.float32) + row_embed[:, None, :] + col_embed[None, :, :]
    pair_normed = (summed * rms_scale(summed) * pair_gain).astype(jnp.bfloat16)
    inner = jax.nn.gelu(
        jnp.dot(pair_normed.reshape(-1, pair_width), pair_w1, preferred_element_type=jnp.float32)
    ).astype(jnp.bfloat16)
    update = jnp.dot(inner, pair_w2, preferred_element_type=jnp.float32).reshape(summed.shape)
    pair_out = (summed + update).astype(jnp.bfloat16)
    return (trunk, pair_out)


def gelu_tanh(x):
    return 0.5 * x * (1.0 + jnp.tanh(math.sqrt(2.0 / math.pi) * (x + 0.044715 * (x * x * x))))


def to_rows(column):
    rows = column.shape[0]
    return jnp.transpose(jnp.broadcast_to(column, (rows, 128)))[:8]


def to_column(tile):
    rows = tile.shape[1]
    return jnp.transpose(jnp.broadcast_to(tile[:1], (128, rows)))[:, :1]


class Sems:
    def __init__(self, ref, limit):
        self.ref, self.limit, self.used = ref, limit, 0

    def take(self, count=1):
        first = self.used
        self.used += count
        assert self.used <= self.limit
        return first


SENDS = 96
RECVS = 96
HALO = 16


def fused_kernel(
    x_ref, cw_hbm, cg_ref, ag_ref, wq_hbm, wk_hbm, wv_hbm, wo_hbm, pw_hbm, pin_ref, pg_ref, w1_ref, w2_ref,
    trunk_ref, pout_ref,
    cw, wq, wk, wv, wo, pw,
    xin, xf, im, acc, accr, q1, q1r, hid, hall, s2, nrm, part, partr,
    qo, ko, vo, qb, kb, vb, ao, at, ot, tin, eb, rowb, colb,
    lsem, ssem, rsem,
):
    s, t, p = lax.axis_index("seq"), lax.axis_index("tp"), lax.axis_index("pr")
    n_seq = lax.axis_size("seq")
    rows = x_ref.shape[0]
    cin = x_ref.shape[1]
    half = hid.shape[1]
    width = 2 * half
    sends, recvs = Sems(ssem, SENDS), Sems(rsem, RECVS)
    pending = []
    f32, bf16 = jnp.float32, jnp.bfloat16

    def remote(src, dst, recv, dev, cond=None):
        copy = pltpu.make_async_remote_copy(
            src_ref=src, dst_ref=dst, send_sem=ssem.at[sends.take()], recv_sem=rsem.at[recv],
            device_id=dev, device_id_type=pl.DeviceIdType.MESH,
        )
        if cond is None:
            copy.start()
        else:
            pl.when(cond)(lambda: copy.start())
        pending.append((copy, cond))

    def arrived(dst, recv, cond=None):
        copy = pltpu.make_async_remote_copy(
            src_ref=dst, dst_ref=dst, send_sem=ssem.at[0], recv_sem=rsem.at[recv],
            device_id={"pr": 1 - p}, device_id_type=pl.DeviceIdType.MESH,
        )
        if cond is None:
            copy.wait_recv()
        else:
            pl.when(cond)(lambda: copy.wait_recv())

    loads = [pltpu.make_async_copy(a, b, lsem.at[i]) for i, (a, b) in enumerate(
        ((cw_hbm, cw), (wq_hbm, wq), (wk_hbm, wk), (wv_hbm, wv), (wo_hbm, wo), (pw_hbm, pw)))]
    for load in loads:
        load.start()

    barrier = pltpu.get_barrier_semaphore()
    for ds in range(n_seq):
        for dt in range(2):
            for dp in range(2):
                if ds or dt or dp:
                    pl.semaphore_signal(
                        barrier, inc=1,
                        device_id={"seq": lax.rem(s + ds, n_seq), "tp": lax.rem(t + dt, 2), "pr": lax.rem(p + dp, 2)},
                        device_id_type=pl.DeviceIdType.MESH)
    pl.semaphore_wait(barrier, 4 * n_seq - 1)

    other_t, other_p = 1 - t, 1 - p
    diag = p == t
    off = p != t

    r_x = recvs.take(4)
    mine = pl.ds(pl.multiple_of(HALO + p * rows, HALO), rows)
    for td in (other_t, t):
        low, high = xin.at[pl.ds(0, HALO)], xin.at[pl.ds(HALO + 2 * rows, HALO)]
        remote(x_ref, xin.at[mine], r_x + p, {"tp": td, "pr": t}, None if td is other_t else off)
        remote(x_ref.at[pl.ds(rows - HALO, HALO)], low, r_x + 2,
               {"seq": lax.rem(s + 1, n_seq), "tp": td, "pr": t}, (p == 1) & (s < n_seq - 1))
        remote(x_ref.at[pl.ds(0, HALO)], high, r_x + 3,
               {"seq": lax.rem(s + n_seq - 1, n_seq), "tp": td, "pr": t}, (p == 0) & (s > 0))

    @pl.when(diag)
    def _():
        xin[mine, :] = x_ref[...]

    @pl.when(s == 0)
    def _():
        xin[pl.ds(0, HALO), :] = jnp.zeros((HALO, cin), bf16)

    @pl.when(s == n_seq - 1)
    def _():
        xin[pl.ds(HALO + 2 * rows, HALO), :] = jnp.zeros((HALO, cin), bf16)

    for q in range(2):
        arrived(xin.at[pl.ds(HALO + q * rows, rows)], r_x + q, off | (p != q))
    arrived(xin.at[pl.ds(0, HALO)], r_x + 2, s > 0)
    arrived(xin.at[pl.ds(HALO + 2 * rows, HALO)], r_x + 3, s < n_seq - 1)

    xf[...] = xin[...].astype(f32)
    taps = im.shape[1] // cin
    for o in range(taps):
        im[:, o * cin:(o + 1) * cin] = xf[pl.ds(HALO - taps // 2 + o, 2 * rows), :].astype(bf16)

    own = pl.ds(pl.multiple_of(p * rows, rows), rows)
    theirs = pl.ds(pl.multiple_of(other_p * rows, rows), rows)
    partner = {"pr": other_p}
    loads[0].wait()
    step = 256
    chunks = half // step
    r_c = recvs.take(chunks)
    for c in range(chunks):
        cols = pl.ds(c * step, step)
        acc[:, cols] = jnp.dot(im[...], cw[:, cols], preferred_element_type=f32)
        remote(acc.at[theirs, cols], accr.at[:, cols], r_c + c, partner)
    square = jnp.zeros((rows, 1), f32)
    for c in range(chunks):
        cols = pl.ds(c * step, step)
        arrived(accr.at[:, cols], r_c + c)
        value = acc[own, cols] + accr[:, cols]
        accr[:, cols] = value
        square = square + jnp.sum(value * value, axis=1, keepdims=True)
    q1[...] = to_rows(square)
    r_q = recvs.take()
    remote(q1, q1r, r_q, {"tp": other_t})
    arrived(q1r, r_q)
    scale = to_column(lax.rsqrt((q1[...] + q1r[...]) / width + EPSILON))

    me4 = t * 2 + p
    r_h = recvs.take(2 * chunks)
    hmine = own
    square = jnp.zeros((rows, 1), f32)
    for c in range(chunks):
        cols = pl.ds(c * step, step)
        rounded = gelu_tanh(accr[:, cols] * scale * cg_ref[:, cols]).astype(bf16)
        hid[:, cols] = rounded
        wide = rounded.astype(f32)
        square = square + jnp.sum(wide * wide, axis=1, keepdims=True)
        remote(hid.at[:, cols], hall.at[hmine, cols], r_h + 2 * c + p, {"tp": other_t, "pr": t})
        remote(hid.at[:, cols], hall.at[hmine, cols], r_h + 2 * c + p, {"pr": t}, off)
    s2[me4] = to_rows(square)
    r_s = recvs.take(4)
    for dt in range(2):
        for dp in range(2):
            if dt or dp:
                remote(s2.at[me4], s2.at[me4], r_s + me4, {"tp": lax.rem(t + dt, 2), "pr": lax.rem(p + dp, 2)})

    @pl.when(diag)
    def _():
        hall[hmine, :] = hid[...]

    for i in range(4):
        arrived(s2.at[i], r_s + i, me4 != i)
    for q in range(2):
        for c in range(chunks):
            arrived(hall.at[pl.ds(q * rows, rows), pl.ds(c * step, step)], r_h + 2 * c + q, off | (p != q))
        scale = to_column(lax.rsqrt((s2[q] + s2[2 + q]) / width + EPSILON))
        block = pl.ds(q * rows, rows)
        nrm[block, :] = (hall[block, :].astype(f32) * scale * ag_ref[p]).astype(bf16)

    for load in loads[1:]:
        load.wait()
    heads = n_seq
    qk = heads * QK
    base_k, base_v, base_q = 0, qk, qk + heads * HV
    plan = [(wk, base_k, c) for c in range(qk // step)] + [
        (wv, base_v, c) for c in range(heads * HV // step)] + [(wq, base_q, c) for c in range(qk // step)]
    r_p = recvs.take(len(plan))
    for i, (w, base, c) in enumerate(plan):
        cols = pl.ds(base + c * step, step)
        part[:, cols] = jnp.dot(nrm[...], w[:, c * step:(c + 1) * step], preferred_element_type=f32)
        remote(part.at[theirs, cols], partr.at[:, cols], r_p + i, partner)

    def finish(i):
        w, base, c = plan[i]
        cols = pl.ds(base + c * step, step)
        arrived(partr.at[:, cols], r_p + i)

    def total(first, count):
        return (part[own, first:first + count] + partr[:, first:first + count]).astype(bf16)

    far = (2, 1, 3) if n_seq == 4 else tuple(range(1, n_seq))

    def scatter(src, dst_of, recv):
        for d in far:
            h = lax.rem(s + d, n_seq)
            remote(src.at[h], dst_of(s), recv + d, {"seq": h})

    r_k, r_v, r_qq = recvs.take(n_seq), recvs.take(n_seq), recvs.take(n_seq)
    n_k, n_v = qk // step, heads * HV // step
    for i in range(n_k):
        finish(i)
    for h in range(heads):
        ko[h] = total(base_k + h * QK, QK)
    scatter(ko, lambda j: kb.at[j, p], r_k)
    kb[s, p] = ko[s]
    for i in range(n_k, n_k + n_v):
        finish(i)
    for h in range(heads):
        vo[h] = total(base_v + h * HV, HV)
    scatter(vo, lambda j: vb.at[j, p], r_v)
    vb[s, p] = vo[s]
    for i in range(n_k + n_v, len(plan)):
        finish(i)
    for h in range(heads):
        qo[h] = total(base_q + h * QK, QK)
    scatter(qo, lambda j: qb.at[j], r_qq)
    qb[s] = qo[s]

    r_k2, r_v2 = recvs.take(n_seq), recvs.take(n_seq)
    near = (0, 1, 3, 2) if n_seq == 4 else tuple(range(n_seq))
    for buf, got, on in ((kb, r_k, r_k2), (vb, r_v, r_v2)):
        for d in near:
            j = lax.rem(s + n_seq - d, n_seq)
            if d:
                arrived(buf.at[j, p], got + d)
            remote(buf.at[j, p], buf.at[j, p], on + d, partner)
    for buf, on in ((kb, r_k2), (vb, r_v2)):
        for d in near:
            j = lax.rem(s + n_seq - d, n_seq)
            arrived(buf.at[j, other_p], on + d)

    factor = 1.0 / math.sqrt(QK)
    r_a, r_a2 = recvs.take(n_seq), recvs.take(n_seq)
    keys_total = 2 * n_seq * rows
    for d in far + (0,):
        j = lax.rem(s + n_seq - d, n_seq)
        if d:
            arrived(qb.at[j], r_qq + d)
        scores = lax.dot_general(
            qb[j], kb[...].reshape(keys_total, QK), (((1,), (1,)), ((), ())), preferred_element_type=f32) * factor
        weights = jnp.exp(scores - jnp.max(scores, axis=1, keepdims=True))
        sums = jnp.sum(weights, axis=1, keepdims=True)
        mixed = jnp.dot(weights.astype(bf16), vb[...].reshape(keys_total, HV), preferred_element_type=f32)
        result = (mixed / sums).astype(bf16)
        if d:
            ao[d] = result
            remote(ao.at[d], at.at[s, p], r_a + d, {"seq": j})
        else:
            at[s, p] = result
    for d in (0,) + far[::-1]:
        h = lax.rem(s + d, n_seq)
        if d:
            arrived(at.at[h, p], r_a + d)
        remote(at.at[h, p], at.at[h, p], r_a2 + d, partner)
    for d in range(n_seq):
        arrived(at.at[lax.rem(s + d, n_seq), other_p], r_a2 + d)

    r_o = recvs.take(2 * chunks)
    for c in range(chunks):
        cols = pl.ds(c * step, step)
        value = jnp.zeros((2 * rows, step), f32)
        for h in range(heads):
            value = value + jnp.dot(
                at[h].reshape(2 * rows, HV), wo[h * HV:(h + 1) * HV, cols], preferred_element_type=f32)
        ot[:, cols] = value.astype(bf16)
        remote(ot.at[theirs, cols], tin.at[t, :, cols], r_o + 2 * c + t, {"tp": p, "pr": other_p})
        remote(ot.at[own, cols], tin.at[t, :, cols], r_o + 2 * c + t, {"tp": p}, off)

        @pl.when(diag)
        def _():
            tin[t, :, cols] = ot[own, cols]

    partial = jnp.zeros((8, 2 * pin_ref.shape[2]), f32)
    groups = rows // POOL
    for c in range(chunks):
        cols = pl.ds(c * step, step)
        for i in range(2):
            arrived(tin.at[i, :, cols], r_o + 2 * c + i, off | (t != i))
        trunk = (hid[:, cols].astype(f32) + (tin[0, :, cols].astype(f32) + tin[1, :, cols].astype(f32))).astype(bf16)
        trunk_ref[:, cols] = trunk
        pooled = jnp.sum(trunk.astype(f32).reshape(groups, POOL, step), axis=1) * (1.0 / POOL)
        first = pooled.astype(bf16)
        rest = pooled - first.astype(f32)
        second = rest.astype(bf16)
        third = (rest - second.astype(f32)).astype(bf16)
        for piece in (third, second, first):
            partial = partial + jnp.dot(piece, pw[c * step:(c + 1) * step, :], preferred_element_type=f32)
    pair = pin_ref.shape[2]
    eb[0] = partial[:, :pair]
    eb[1] = partial[:, pair:]
    r_r, r_e = recvs.take(2), recvs.take(8)
    remote(eb.at[0], rowb.at[t], r_r + t, {"tp": p, "pr": other_p})
    remote(eb.at[0], rowb.at[t], r_r + t, {"tp": p}, off)

    @pl.when(diag)
    def _():
        rowb[t] = eb[0]

    side = s // 2
    slot = lax.rem(s, 2) * 2 + p
    for d in far + (0,):
        for dt in range(2):
            remote(eb.at[1], colb.at[t, slot], r_e + t * 4 + slot,
                   {"seq": lax.rem(s + d, n_seq), "tp": lax.rem(t + dt, 2), "pr": side},
                   (p != side) if d == 0 and dt == 0 else None)

    @pl.when(p == side)
    def _():
        colb[t, slot] = eb[1]

    for i in range(2):
        arrived(rowb.at[i], r_r + i, off | (t != i))
    for i in range(2):
        for k in range(4):
            arrived(colb.at[i, k], r_e + i * 4 + k, (t != i) | (slot != k) | (p != side))
    row_embed = (rowb[0] + rowb[1]).astype(bf16).astype(f32)
    col_embed = (colb[0] + colb[1]).reshape(4 * groups, pair).astype(bf16).astype(f32)
    summed = pin_ref[...].astype(f32) + row_embed[:, None, :] + col_embed[None, :, :]
    flat = summed.reshape(-1, pair)
    inv = lax.rsqrt(jnp.mean(flat * flat, axis=1, keepdims=True) + EPSILON)
    normal = (flat * inv * pg_ref[...]).astype(bf16)
    inner = gelu_tanh(jnp.dot(normal, w1_ref[...], preferred_element_type=f32)).astype(bf16)
    update = jnp.dot(inner, w2_ref[...], preferred_element_type=f32)
    pout_ref[...] = (flat + update).astype(bf16).reshape(pout_ref.shape)

    for copy, cond in pending:
        if cond is None:
            copy.wait_send()
        else:
            pl.when(cond)(lambda copy=copy: copy.wait_send())


def fused(dna_feats, conv_w, conv_gain, attn_gain, wq, wk, wv, wo, pair_w, pair_in, pair_gain, pair_w1, pair_w2):
    rows, cin = dna_feats.shape
    taps, _, half = conv_w.shape
    heads = lax.axis_size("seq")
    width = half * 2
    bf16, f32 = jnp.bfloat16, jnp.float32
    vmem = pl.BlockSpec(memory_space=pltpu.VMEM)
    hbm = pl.BlockSpec(memory_space=pl.ANY)
    flat_conv = conv_w.reshape(taps * cin, half)
    total = heads * (2 * QK + HV)
    pair = pair_in.shape[2]
    groups = rows // POOL
    v = pltpu.VMEM
    scratch = [
        v(flat_conv.shape, bf16), v(wq.shape, bf16), v(wk.shape, bf16), v(wv.shape, bf16), v(wo.shape, bf16),
        v(pair_w.shape, bf16),
        v((2 * rows + 2 * HALO, cin), bf16), v((2 * rows + 2 * HALO, cin), f32), v((2 * rows, taps * cin), bf16),
        v((2 * rows, half), f32), v((rows, half), f32), v((8, rows), f32), v((8, rows), f32),
        v((rows, half), bf16), v((2 * rows, half), bf16), v((4, 8, rows), f32), v((2 * rows, half), bf16),
        v((2 * rows, total), f32), v((rows, total), f32),
        v((heads, rows, QK), bf16), v((heads, rows, QK), bf16), v((heads, rows, HV), bf16),
        v((heads, rows, QK), bf16), v((heads, 2, rows, QK), bf16), v((heads, 2, rows, HV), bf16),
        v((heads, rows, HV), bf16), v((heads, 2, rows, HV), bf16),
        v((2 * rows, half), bf16), v((2, rows, half), bf16),
        v((2, groups, pair), f32), v((2, groups, pair), f32), v((2, 4, groups, pair), f32),
        pltpu.SemaphoreType.DMA((8,)), pltpu.SemaphoreType.DMA((SENDS,)), pltpu.SemaphoreType.DMA((RECVS,)),
    ]
    return pl.pallas_call(
        fused_kernel,
        out_shape=(jax.ShapeDtypeStruct((rows, half), bf16), jax.ShapeDtypeStruct(pair_in.shape, bf16)),
        in_specs=[vmem, hbm, vmem, vmem, hbm, hbm, hbm, hbm, hbm, vmem, vmem, vmem, vmem],
        out_specs=(vmem, vmem),
        scratch_shapes=scratch,
        compiler_params=pltpu.CompilerParams(
            collective_id=0, has_side_effects=True, vmem_limit_bytes=60 * 1024 * 1024),
    )(dna_feats, flat_conv, conv_gain.reshape(1, half), attn_gain.reshape(2, 1, half), wq, wk, wv, wo, pair_w,
      pair_in, pair_gain.reshape(1, pair), pair_w1, pair_w2)


def block(*arrays):
    dna_feats, conv_w, wq = arrays[0], arrays[1], arrays[4]
    n_seq, n_tp, n_pr = (lax.axis_size(a) for a in ("seq", "tp", "pr"))
    fits = (
        n_tp == 2 and n_pr == 2 and n_seq == 4 and wq.shape[1] == n_seq * QK
        and dna_feats.shape[0] == 128 and conv_w.shape[1] == dna_feats.shape[1]
        and arrays[3].shape[0] == 2 * conv_w.shape[2] and conv_w.shape[2] % 256 == 0
        and arrays[9].shape[0] * POOL == dna_feats.shape[0]
    )
    return fused(*arrays) if fits else local(*arrays)


def solution(mesh):
    in_specs = (
        P(("grp", "seq", "pr"), "tp"),
        P(None, "pr", "tp"),
        P("tp"),
        P(),
        P("pr", "tp"),
        P("pr", "tp"),
        P("pr", "tp"),
        P("tp", "pr"),
        P("tp", None),
        P(("grp", "seq", "tp"), "pr", None),
        P(),
        P(),
        P(),
    )
    out_specs = (P(("grp", "seq", "pr"), "tp"), P(("grp", "seq", "tp"), "pr", None))
    return jax.shard_map(block, mesh=mesh, in_specs=in_specs, out_specs=out_specs, check_vma=False)
```

```python
import math

import jax
import jax.numpy as jnp
from jax import lax
from jax.experimental import pallas as pl
from jax.experimental.pallas import tpu as pltpu
from jax.sharding import PartitionSpec as P

QK = 128
HV = 192
POOL = 16


EPSILON = 1e-06


def extended(value, sides, width):
    for axis, dim in sides:
        devices, length = (lax.axis_size(axis), value.shape[dim])
        up = [(i, (i + 1) % devices) for i in range(devices - 1)]
        down = [(j, i) for i, j in up]
        last = lax.slice_in_dim(value, length - width, length, axis=dim)
        first = lax.slice_in_dim(value, 0, width, axis=dim)
        before = lax.ppermute(last, axis, up)
        after = lax.ppermute(first, axis, down)
        value = jnp.concatenate([before, value, after], axis=dim)
    return value


def rms_scale(values):
    return lax.rsqrt(jnp.mean(values * values, axis=-1, keepdims=True) + EPSILON)


def attention_start(query_block):
    head_count = query_block.shape[1]
    row_count = query_block.shape[0]
    highest = jnp.full((head_count, row_count), -1e30, jnp.float32)
    totals = jnp.zeros((head_count, row_count), jnp.float32)
    mixed = jnp.zeros((row_count, head_count, HV), jnp.float32)
    return (highest, totals, mixed)


def attention_step(query_block, carry, pieces):
    factor = 1.0 / math.sqrt(QK)
    highest, totals, mixed = carry
    key_piece, value_piece = pieces
    scores = (
        jnp.einsum("qhd,khd->hqk", query_block, key_piece, preferred_element_type=jnp.float32)
        * factor
    )
    new_high = jnp.maximum(highest, jnp.max(scores, axis=-1))
    weights = jnp.exp(scores - new_high[:, :, None])
    totals = jnp.sum(weights, axis=-1)
    added = jnp.einsum(
        "hqk,khd->qhd",
        weights.astype(jnp.bfloat16),
        value_piece,
        preferred_element_type=jnp.float32,
    )
    mixed = added
    return (new_high, totals, mixed)


def attention_finish(carry):
    highest, totals, mixed = carry
    return (mixed / jnp.transpose(totals)[:, :, None]).astype(jnp.bfloat16)


def local(
    dna_feats,
    conv_w,
    conv_gain,
    attn_gain,
    wq,
    wk,
    wv,
    wo,
    pair_w,
    pair_in,
    pair_gain,
    pair_w1,
    pair_w2,
):
    row_count = dna_feats.shape[0]
    reach = conv_w.shape[0] // 2
    rimmed = extended(dna_feats, ((("seq", "pr"), 0),), reach)
    channels = lax.all_gather(rimmed, "tp", axis=1, tiled=True)
    conv_empty = jnp.zeros((row_count, conv_w.shape[2]), jnp.float32)
    total = conv_empty
    piece = lax.all_gather(conv_w, "pr", axis=1, tiled=True)
    sliced = channels
    for offset in range(piece.shape[0]):
        total = total + jnp.dot(
            sliced[offset : offset + row_count], piece[offset], preferred_element_type=jnp.float32
        )
    squares = lax.psum(jnp.sum(total * total, axis=1, keepdims=True), "tp")
    model_width = total.shape[1] * lax.axis_size("tp")
    hidden_conv = jax.nn.gelu(
        total * lax.rsqrt(squares / model_width + EPSILON) * conv_gain
    ).astype(jnp.bfloat16)
    trunk_full = lax.all_gather(hidden_conv, "tp", axis=1, tiled=True)
    trunk_wide = trunk_full.astype(jnp.float32)
    normed = (trunk_wide * rms_scale(trunk_wide) * attn_gain).astype(jnp.bfloat16)
    query_width = wq.shape[1]
    pieces = (
        lax.all_gather(wq, "pr", axis=0, tiled=True),
        lax.all_gather(wk, "pr", axis=0, tiled=True),
        lax.all_gather(wv, "pr", axis=0, tiled=True),
    )
    sliced = normed
    query_sum, key_sum, value_sum = tuple(
        (jnp.dot(sliced, piece, preferred_element_type=jnp.float32) for piece in pieces)
    )
    head_count = query_width // QK
    queries = query_sum.astype(jnp.bfloat16).reshape(row_count, head_count, QK)
    keys_local = key_sum.astype(jnp.bfloat16).reshape(row_count, head_count, QK)
    values_local = value_sum.astype(jnp.bfloat16).reshape(row_count, head_count, HV)
    moved_query, moved_keys, moved_values = (
        lax.all_to_all(queries, "pr", split_axis=1, concat_axis=0, tiled=True),
        lax.all_to_all(keys_local, "pr", split_axis=1, concat_axis=0, tiled=True),
        lax.all_to_all(values_local, "pr", split_axis=1, concat_axis=0, tiled=True),
    )
    carried = attention_step(
        moved_query,
        attention_start(moved_query),
        (
            lax.all_gather(moved_keys, "seq", axis=0, tiled=True),
            lax.all_gather(moved_values, "seq", axis=0, tiled=True),
        ),
    )
    attended = lax.all_to_all(
        attention_finish(carried), "pr", split_axis=0, concat_axis=1, tiled=True
    )
    attended_flat = attended.reshape(row_count, head_count * HV)
    head_terms = jnp.dot(
        attended_flat,
        lax.all_gather(wo, "pr", axis=1, tiled=True),
        preferred_element_type=jnp.float32,
    )
    own_share = lax.psum_scatter(
        head_terms.astype(jnp.bfloat16), "tp", scatter_dimension=1, tiled=True
    ).astype(jnp.float32)
    trunk = (hidden_conv.astype(jnp.float32) + own_share).astype(jnp.bfloat16)
    pooled = trunk.astype(jnp.float32).reshape(row_count // POOL, POOL, -1).mean(axis=1)
    partial_embed = jnp.dot(pooled, pair_w.astype(jnp.float32), precision=lax.Precision.HIGHEST)
    embedded = lax.psum(partial_embed, "tp").astype(jnp.bfloat16)
    every_embed = lax.all_gather(embedded, ("seq", "pr"), axis=0, tiled=True)
    pair_rows = pair_in.shape[0]
    pair_cols = pair_in.shape[1]
    pair_width = pair_in.shape[2]
    row_first = lax.axis_index(("seq", "tp")) * pair_rows
    col_first = lax.axis_index("pr") * pair_cols
    row_embed = lax.dynamic_slice_in_dim(every_embed, row_first, pair_rows, 0)[
        :, :pair_width
    ].astype(jnp.float32)
    col_embed = lax.dynamic_slice_in_dim(every_embed, col_first, pair_cols, 0)[
        :, pair_width:
    ].astype(jnp.float32)
    summed = pair_in.astype(jnp.float32) + row_embed[:, None, :] + col_embed[None, :, :]
    pair_normed = (summed * rms_scale(summed) * pair_gain).astype(jnp.bfloat16)
    inner = jax.nn.gelu(
        jnp.dot(pair_normed.reshape(-1, pair_width), pair_w1, preferred_element_type=jnp.float32)
    ).astype(jnp.bfloat16)
    update = jnp.dot(inner, pair_w2, preferred_element_type=jnp.float32).reshape(summed.shape)
    pair_out = (summed + update).astype(jnp.bfloat16)
    return (trunk, pair_out)


def gelu_tanh(x):
    return 0.5 * x * (1.0 + jnp.tanh(math.sqrt(2.0 / math.pi) * (x + 0.044715 * (x * x * x))))


def to_rows(column):
    rows = column.shape[0]
    return jnp.transpose(jnp.broadcast_to(column, (rows, 128)))[:8]


def to_column(tile):
    rows = tile.shape[1]
    return jnp.transpose(jnp.broadcast_to(tile[:1], (128, rows)))[:, :1]


class Sems:
    def __init__(self, ref, limit):
        self.ref, self.limit, self.used = ref, limit, 0

    def take(self, count=1):
        first = self.used
        self.used += count
        assert self.used <= self.limit
        return first


def fold(ref, value):
    rows, extra = value.shape[0], value.shape[1] - 128
    ref[pl.ds(0, rows), :] = value[:, :128]
    depth = rows * extra // 128
    for i in range(128 // extra):
        ref[pl.ds(rows, depth), i * extra:(i + 1) * extra] = value[i * depth:(i + 1) * depth, 128:]


def unfold(ref, out):
    rows, extra = out.shape[0], out.shape[1] - 128
    out[:, :128] = ref[pl.ds(0, rows), :]
    depth = rows * extra // 128
    for i in range(128 // extra):
        out[pl.ds(i * depth, depth), 128:] = ref[pl.ds(rows, depth), i * extra:(i + 1) * extra]


SENDS = 96
RECVS = 96
HALO = 16


def fused_kernel(
    x_ref, cw_hbm, cg_ref, ag_ref, wq_hbm, wk_hbm, wv_hbm, wo_hbm, pw_hbm, pin_ref, pg_ref, w1_ref, w2_ref,
    trunk_ref, pout_ref,
    cw, wq, wk, wv, wo, pw,
    xin, xf, im, acc, accr, q1, q1r, hid, hall, s2, nrm, part, partr,
    qo, ko, vo, qb, kb, vb, ao, at, vf, af, ot, tin, eb, rowb, colb,
    lsem, ssem, rsem,
):
    s, t, p = lax.axis_index("seq"), lax.axis_index("tp"), lax.axis_index("pr")
    n_seq = lax.axis_size("seq")
    rows = x_ref.shape[0]
    cin = x_ref.shape[1]
    half = hid.shape[1]
    width = 2 * half
    sends, recvs = Sems(ssem, SENDS), Sems(rsem, RECVS)
    pending = []
    f32, bf16 = jnp.float32, jnp.bfloat16

    def remote(src, dst, recv, dev, cond=None):
        copy = pltpu.make_async_remote_copy(
            src_ref=src, dst_ref=dst, send_sem=ssem.at[sends.take()], recv_sem=rsem.at[recv],
            device_id=dev, device_id_type=pl.DeviceIdType.MESH,
        )
        if cond is None:
            copy.start()
        else:
            pl.when(cond)(lambda: copy.start())
        pending.append((copy, cond))

    def arrived(dst, recv, cond=None):
        copy = pltpu.make_async_remote_copy(
            src_ref=dst, dst_ref=dst, send_sem=ssem.at[0], recv_sem=rsem.at[recv],
            device_id={"pr": 1 - p}, device_id_type=pl.DeviceIdType.MESH,
        )
        if cond is None:
            copy.wait_recv()
        else:
            pl.when(cond)(lambda: copy.wait_recv())

    loads = [pltpu.make_async_copy(a, b, lsem.at[i]) for i, (a, b) in enumerate(
        ((cw_hbm, cw), (wq_hbm, wq), (wk_hbm, wk), (wv_hbm, wv), (wo_hbm, wo), (pw_hbm, pw)))]
    for load in loads:
        load.start()

    barrier = pltpu.get_barrier_semaphore()
    for ds in range(n_seq):
        for dt in range(2):
            for dp in range(2):
                if ds or dt or dp:
                    pl.semaphore_signal(
                        barrier, inc=1,
                        device_id={"seq": lax.rem(s + ds, n_seq), "tp": lax.rem(t + dt, 2), "pr": lax.rem(p + dp, 2)},
                        device_id_type=pl.DeviceIdType.MESH)
    pl.semaphore_wait(barrier, 4 * n_seq - 1)

    other_t, other_p = 1 - t, 1 - p
    diag = p == t
    off = p != t

    r_x = recvs.take(4)
    mine = pl.ds(pl.multiple_of(HALO + p * rows, HALO), rows)
    for td in (other_t, t):
        low, high = xin.at[pl.ds(0, HALO)], xin.at[pl.ds(HALO + 2 * rows, HALO)]
        remote(x_ref, xin.at[mine], r_x + p, {"tp": td, "pr": t}, None if td is other_t else off)
        remote(x_ref.at[pl.ds(rows - HALO, HALO)], low, r_x + 2,
               {"seq": lax.rem(s + 1, n_seq), "tp": td, "pr": t}, (p == 1) & (s < n_seq - 1))
        remote(x_ref.at[pl.ds(0, HALO)], high, r_x + 3,
               {"seq": lax.rem(s + n_seq - 1, n_seq), "tp": td, "pr": t}, (p == 0) & (s > 0))

    @pl.when(diag)
    def _():
        xin[mine, :] = x_ref[...]

    @pl.when(s == 0)
    def _():
        xin[pl.ds(0, HALO), :] = jnp.zeros((HALO, cin), bf16)

    @pl.when(s == n_seq - 1)
    def _():
        xin[pl.ds(HALO + 2 * rows, HALO), :] = jnp.zeros((HALO, cin), bf16)

    for q in range(2):
        arrived(xin.at[pl.ds(HALO + q * rows, rows)], r_x + q, off | (p != q))
    arrived(xin.at[pl.ds(0, HALO)], r_x + 2, s > 0)
    arrived(xin.at[pl.ds(HALO + 2 * rows, HALO)], r_x + 3, s < n_seq - 1)

    xf[...] = xin[...].astype(f32)
    taps = im.shape[1] // cin
    for o in range(taps):
        im[:, o * cin:(o + 1) * cin] = xf[pl.ds(HALO - taps // 2 + o, 2 * rows), :].astype(bf16)

    own = pl.ds(pl.multiple_of(p * rows, rows), rows)
    theirs = pl.ds(pl.multiple_of(other_p * rows, rows), rows)
    partner = {"pr": other_p}
    loads[0].wait()
    step = 256
    chunks = half // step
    r_c = recvs.take(chunks)
    for c in range(chunks):
        cols = pl.ds(c * step, step)
        acc[:, cols] = jnp.dot(im[...], cw[:, cols], preferred_element_type=f32)
        remote(acc.at[theirs, cols], accr.at[:, cols], r_c + c, partner)
    square = jnp.zeros((rows, 1), f32)
    for c in range(chunks):
        cols = pl.ds(c * step, step)
        arrived(accr.at[:, cols], r_c + c)
        value = acc[own, cols] + accr[:, cols]
        accr[:, cols] = value
        square = square + jnp.sum(value * value, axis=1, keepdims=True)
    q1[...] = to_rows(square)
    r_q = recvs.take()
    remote(q1, q1r, r_q, {"tp": other_t})
    arrived(q1r, r_q)
    scale = to_column(lax.rsqrt((q1[...] + q1r[...]) / width + EPSILON))

    me4 = t * 2 + p
    r_h = recvs.take(2 * chunks)
    hmine = own
    square = jnp.zeros((rows, 1), f32)
    for c in range(chunks):
        cols = pl.ds(c * step, step)
        rounded = gelu_tanh(accr[:, cols] * scale * cg_ref[cols][None, :]).astype(bf16)
        hid[:, cols] = rounded
        wide = rounded.astype(f32)
        square = square + jnp.sum(wide * wide, axis=1, keepdims=True)
        remote(hid.at[:, cols], hall.at[hmine, cols], r_h + 2 * c + p, {"tp": other_t, "pr": t})
        remote(hid.at[:, cols], hall.at[hmine, cols], r_h + 2 * c + p, {"pr": t}, off)
    s2[me4] = to_rows(square)
    r_s = recvs.take(4)
    for dt in range(2):
        for dp in range(2):
            if dt or dp:
                remote(s2.at[me4], s2.at[me4], r_s + me4, {"tp": lax.rem(t + dt, 2), "pr": lax.rem(p + dp, 2)})

    @pl.when(diag)
    def _():
        hall[hmine, :] = hid[...]

    gain = jnp.where(p == 0, ag_ref[pl.ds(0, half)][None, :], ag_ref[pl.ds(half, half)][None, :])
    for i in range(4):
        arrived(s2.at[i], r_s + i, me4 != i)
    for q in range(2):
        for c in range(chunks):
            arrived(hall.at[pl.ds(q * rows, rows), pl.ds(c * step, step)], r_h + 2 * c + q, off | (p != q))
        scale = to_column(lax.rsqrt((s2[q] + s2[2 + q]) / width + EPSILON))
        block = pl.ds(q * rows, rows)
        nrm[block, :] = (hall[block, :].astype(f32) * scale * gain).astype(bf16)

    for load in loads[1:]:
        load.wait()
    heads = n_seq
    qk = heads * QK
    base_k, base_v, base_q = 0, qk, qk + heads * HV
    plan = [(wk, base_k, c) for c in range(qk // step)] + [
        (wv, base_v, c) for c in range(heads * HV // step)] + [(wq, base_q, c) for c in range(qk // step)]
    r_p = recvs.take(len(plan))
    def multiply(i):
        w, base, c = plan[i]
        cols = pl.ds(base + c * step, step)
        part[:, cols] = jnp.dot(nrm[...], w[:, c * step:(c + 1) * step], preferred_element_type=f32)
        remote(part.at[theirs, cols], partr.at[:, cols], r_p + i, partner)

    def finish(i):
        w, base, c = plan[i]
        cols = pl.ds(base + c * step, step)
        arrived(partr.at[:, cols], r_p + i)

    def total(first, count):
        return (part[own, first:first + count] + partr[:, first:first + count]).astype(bf16)

    far = (2, 1, 3) if n_seq == 4 else tuple(range(1, n_seq))

    def scatter(src, dst_of, recv):
        for d in far:
            h = lax.rem(s + d, n_seq)
            remote(src.at[h], dst_of(s), recv + d, {"seq": h})

    r_k, r_v, r_qq = recvs.take(n_seq), recvs.take(n_seq), recvs.take(n_seq)
    n_k, n_v = qk // step, heads * HV // step
    last_k, last_v = n_k, n_k + n_v
    for i in range(last_k + 1):
        multiply(i)
    for i in range(last_k):
        finish(i)
    for h in range(heads):
        ko[h] = total(base_k + h * QK, QK)
    scatter(ko, lambda j: kb.at[j, p], r_k)
    kb[s, p] = ko[s]
    for i in range(last_k + 1, last_v + 1):
        multiply(i)
    for i in range(last_k, last_v):
        finish(i)
    for h in range(heads):
        fold(vo.at[h], total(base_v + h * HV, HV))
    scatter(vo, lambda j: vb.at[j, p], r_v)
    vb[s, p] = vo[s]
    for i in range(last_v + 1, len(plan)):
        multiply(i)
    for i in range(last_v, len(plan)):
        finish(i)
    for h in range(heads):
        qo[h] = total(base_q + h * QK, QK)
    scatter(qo, lambda j: qb.at[j], r_qq)
    qb[s] = qo[s]

    r_k2, r_v2 = recvs.take(n_seq), recvs.take(n_seq)
    near = (0, 1, 3, 2) if n_seq == 4 else tuple(range(n_seq))
    for buf, got, on in ((kb, r_k, r_k2), (vb, r_v, r_v2)):
        for d in near:
            j = lax.rem(s + n_seq - d, n_seq)
            if d:
                arrived(buf.at[j, p], got + d)
            remote(buf.at[j, p], buf.at[j, p], on + d, partner)
    for buf, on in ((kb, r_k2), (vb, r_v2)):
        for d in near:
            j = lax.rem(s + n_seq - d, n_seq)
            arrived(buf.at[j, other_p], on + d)

    factor = 1.0 / math.sqrt(QK)
    r_a, r_a2 = recvs.take(n_seq), recvs.take(n_seq)
    keys_total = 2 * n_seq * rows
    for j in range(n_seq):
        for q in range(2):
            unfold(vb.at[j, q], vf.at[j, q])
    turns = far + (0,)
    for first in range(0, n_seq, 2):
        pair_of = turns[first:first + 2]
        blocks = [lax.rem(s + n_seq - d, n_seq) for d in pair_of]
        for d, j in zip(pair_of, blocks):
            if d:
                arrived(qb.at[j], r_qq + d)
        scores = lax.dot_general(
            jnp.concatenate([qb[j] for j in blocks], axis=0), kb[...].reshape(keys_total, QK),
            (((1,), (1,)), ((), ())), preferred_element_type=f32) * factor
        weights = jnp.exp(scores - jnp.max(scores, axis=1, keepdims=True))
        sums = jnp.sum(weights, axis=1, keepdims=True)
        mixed = jnp.dot(weights.astype(bf16), vf[...].reshape(keys_total, HV), preferred_element_type=f32)
        result = (mixed / sums).astype(bf16)
        for i, (d, j) in enumerate(zip(pair_of, blocks)):
            piece = result[i * rows:(i + 1) * rows]
            if d:
                fold(ao.at[d], piece)
                remote(ao.at[d], at.at[s, p], r_a + d, {"seq": j})
            else:
                fold(at.at[s, p], piece)
    for d in (0,) + far[::-1]:
        h = lax.rem(s + d, n_seq)
        if d:
            arrived(at.at[h, p], r_a + d)
        remote(at.at[h, p], at.at[h, p], r_a2 + d, partner)
    for d in range(n_seq):
        arrived(at.at[lax.rem(s + d, n_seq), other_p], r_a2 + d)

    for h in range(heads):
        for q in range(2):
            unfold(at.at[h, q], af.at[h, q])
    r_o = recvs.take(2 * chunks)
    for c in range(chunks):
        cols = pl.ds(c * step, step)
        value = jnp.zeros((2 * rows, step), f32)
        for h in range(heads):
            value = value + jnp.dot(
                af[h].reshape(2 * rows, HV), wo[h * HV:(h + 1) * HV, cols], preferred_element_type=f32)
        ot[:, cols] = value.astype(bf16)
        remote(ot.at[theirs, cols], tin.at[t, :, cols], r_o + 2 * c + t, {"tp": p, "pr": other_p})
        remote(ot.at[own, cols], tin.at[t, :, cols], r_o + 2 * c + t, {"tp": p}, off)

        @pl.when(diag)
        def _():
            tin[t, :, cols] = ot[own, cols]

    partial = jnp.zeros((8, 2 * pin_ref.shape[2]), f32)
    groups = rows // POOL
    for c in range(chunks):
        cols = pl.ds(c * step, step)
        for i in range(2):
            arrived(tin.at[i, :, cols], r_o + 2 * c + i, off | (t != i))
        trunk = (hid[:, cols].astype(f32) + (tin[0, :, cols].astype(f32) + tin[1, :, cols].astype(f32))).astype(bf16)
        trunk_ref[:, cols] = trunk
        pooled = jnp.sum(trunk.astype(f32).reshape(groups, POOL, step), axis=1) * (1.0 / POOL)
        first = pooled.astype(bf16)
        rest = pooled - first.astype(f32)
        second = rest.astype(bf16)
        third = (rest - second.astype(f32)).astype(bf16)
        for piece in (third, second, first):
            partial = partial + jnp.dot(piece, pw[c * step:(c + 1) * step, :], preferred_element_type=f32)
    pair = pin_ref.shape[2]
    eb[0] = partial[:, :pair]
    eb[1] = partial[:, pair:]
    r_r, r_e = recvs.take(2), recvs.take(8)
    remote(eb.at[0], rowb.at[t], r_r + t, {"tp": p, "pr": other_p})
    remote(eb.at[0], rowb.at[t], r_r + t, {"tp": p}, off)

    @pl.when(diag)
    def _():
        rowb[t] = eb[0]

    side = s // 2
    slot = lax.rem(s, 2) * 2 + p
    for d in far + (0,):
        for dt in range(2):
            remote(eb.at[1], colb.at[t, slot], r_e + t * 4 + slot,
                   {"seq": lax.rem(s + d, n_seq), "tp": lax.rem(t + dt, 2), "pr": side},
                   (p != side) if d == 0 and dt == 0 else None)

    @pl.when(p == side)
    def _():
        colb[t, slot] = eb[1]

    for i in range(2):
        arrived(rowb.at[i], r_r + i, off | (t != i))
    for i in range(2):
        for k in range(4):
            arrived(colb.at[i, k], r_e + i * 4 + k, (t != i) | (slot != k) | (p != side))
    row_embed = (rowb[0] + rowb[1]).astype(bf16).astype(f32)
    col_embed = (colb[0] + colb[1]).reshape(4 * groups, pair).astype(bf16).astype(f32)
    summed = pin_ref[...].astype(f32) + row_embed[:, None, :] + col_embed[None, :, :]
    flat = summed.reshape(-1, pair)
    inv = lax.rsqrt(jnp.mean(flat * flat, axis=1, keepdims=True) + EPSILON)
    normal = (flat * inv * pg_ref[...]).astype(bf16)
    inner = gelu_tanh(jnp.dot(normal, w1_ref[...], preferred_element_type=f32)).astype(bf16)
    update = jnp.dot(inner, w2_ref[...], preferred_element_type=f32)
    pout_ref[...] = (flat + update).astype(bf16).reshape(pout_ref.shape)

    for copy, cond in pending:
        if cond is None:
            copy.wait_send()
        else:
            pl.when(cond)(lambda copy=copy: copy.wait_send())


def fused(dna_feats, conv_w, conv_gain, attn_gain, wq, wk, wv, wo, pair_w, pair_in, pair_gain, pair_w1, pair_w2):
    rows, cin = dna_feats.shape
    taps, _, half = conv_w.shape
    heads = lax.axis_size("seq")
    width = half * 2
    bf16, f32 = jnp.bfloat16, jnp.float32
    vmem = pl.BlockSpec(memory_space=pltpu.VMEM)
    hbm = pl.BlockSpec(memory_space=pltpu.HBM)
    flat_conv = conv_w.reshape(taps * cin, half)
    total = heads * (2 * QK + HV)
    pair = pair_in.shape[2]
    groups = rows // POOL
    packed = rows * HV // 128
    v = pltpu.VMEM
    scratch = [
        v(flat_conv.shape, bf16), v(wq.shape, bf16), v(wk.shape, bf16), v(wv.shape, bf16), v(wo.shape, bf16),
        v(pair_w.shape, bf16),
        v((2 * rows + 2 * HALO, cin), bf16), v((2 * rows + 2 * HALO, cin), f32), v((2 * rows, taps * cin), bf16),
        v((2 * rows, half), f32), v((rows, half), f32), v((8, rows), f32), v((8, rows), f32),
        v((rows, half), bf16), v((2 * rows, half), bf16), v((4, 8, rows), f32), v((2 * rows, half), bf16),
        v((2 * rows, total), f32), v((rows, total), f32),
        v((heads, rows, QK), bf16), v((heads, rows, QK), bf16), v((heads, packed, 128), bf16),
        v((heads, rows, QK), bf16), v((heads, 2, rows, QK), bf16), v((heads, 2, packed, 128), bf16),
        v((heads, packed, 128), bf16), v((heads, 2, packed, 128), bf16),
        v((heads, 2, rows, HV), bf16), v((heads, 2, rows, HV), bf16),
        v((2 * rows, half), bf16), v((2, rows, half), bf16),
        v((2, groups, pair), f32), v((2, groups, pair), f32), v((2, 4, groups, pair), f32),
        pltpu.SemaphoreType.DMA((8,)), pltpu.SemaphoreType.DMA((SENDS,)), pltpu.SemaphoreType.DMA((RECVS,)),
    ]
    return pl.pallas_call(
        fused_kernel,
        out_shape=(jax.ShapeDtypeStruct((rows, half), bf16), jax.ShapeDtypeStruct(pair_in.shape, bf16)),
        in_specs=[vmem, hbm, vmem, vmem, hbm, hbm, hbm, hbm, hbm, vmem, vmem, vmem, vmem],
        out_specs=(vmem, vmem),
        scratch_shapes=scratch,
        compiler_params=pltpu.CompilerParams(
            collective_id=0, has_side_effects=True, vmem_limit_bytes=32 * 1024 * 1024),
    )(dna_feats, flat_conv, conv_gain, attn_gain, wq, wk, wv, wo, pair_w,
      pair_in, pair_gain.reshape(1, pair), pair_w1, pair_w2)


def block(*arrays):
    dna_feats, conv_w, wq = arrays[0], arrays[1], arrays[4]
    n_seq, n_tp, n_pr = (lax.axis_size(a) for a in ("seq", "tp", "pr"))
    fits = (
        n_tp == 2 and n_pr == 2 and n_seq == 4 and wq.shape[1] == n_seq * QK
        and dna_feats.shape[0] == 128 and conv_w.shape[1] == dna_feats.shape[1]
        and arrays[3].shape[0] == 2 * conv_w.shape[2] and conv_w.shape[2] % 256 == 0
        and arrays[9].shape[0] * POOL == dna_feats.shape[0]
    )
    return fused(*arrays) if fits else local(*arrays)


def solution(mesh):
    in_specs = (
        P(("grp", "seq", "pr"), "tp"),
        P(None, "pr", "tp"),
        P("tp"),
        P(),
        P("pr", "tp"),
        P("pr", "tp"),
        P("pr", "tp"),
        P("tp", "pr"),
        P("tp", None),
        P(("grp", "seq", "tp"), "pr", None),
        P(),
        P(),
        P(),
    )
    out_specs = (P(("grp", "seq", "pr"), "tp"), P(("grp", "seq", "tp"), "pr", None))
    return jax.shard_map(block, mesh=mesh, in_specs=in_specs, out_specs=out_specs, check_vma=False)
```

```python
import math

import jax
import jax.numpy as jnp
from jax import lax
from jax.experimental import pallas as pl
from jax.experimental.pallas import tpu as pltpu
from jax.sharding import PartitionSpec as P

QK = 128
HV = 192
POOL = 16


EPSILON = 1e-06


def extended(value, sides, width):
    for axis, dim in sides:
        devices, length = (lax.axis_size(axis), value.shape[dim])
        up = [(i, (i + 1) % devices) for i in range(devices - 1)]
        down = [(j, i) for i, j in up]
        last = lax.slice_in_dim(value, length - width, length, axis=dim)
        first = lax.slice_in_dim(value, 0, width, axis=dim)
        before = lax.ppermute(last, axis, up)
        after = lax.ppermute(first, axis, down)
        value = jnp.concatenate([before, value, after], axis=dim)
    return value


def rms_scale(values):
    return lax.rsqrt(jnp.mean(values * values, axis=-1, keepdims=True) + EPSILON)


def attention_start(query_block):
    head_count = query_block.shape[1]
    row_count = query_block.shape[0]
    highest = jnp.full((head_count, row_count), -1e30, jnp.float32)
    totals = jnp.zeros((head_count, row_count), jnp.float32)
    mixed = jnp.zeros((row_count, head_count, HV), jnp.float32)
    return (highest, totals, mixed)


def attention_step(query_block, carry, pieces):
    factor = 1.0 / math.sqrt(QK)
    highest, totals, mixed = carry
    key_piece, value_piece = pieces
    scores = (
        jnp.einsum("qhd,khd->hqk", query_block, key_piece, preferred_element_type=jnp.float32)
        * factor
    )
    new_high = jnp.maximum(highest, jnp.max(scores, axis=-1))
    weights = jnp.exp(scores - new_high[:, :, None])
    totals = jnp.sum(weights, axis=-1)
    added = jnp.einsum(
        "hqk,khd->qhd",
        weights.astype(jnp.bfloat16),
        value_piece,
        preferred_element_type=jnp.float32,
    )
    mixed = added
    return (new_high, totals, mixed)


def attention_finish(carry):
    highest, totals, mixed = carry
    return (mixed / jnp.transpose(totals)[:, :, None]).astype(jnp.bfloat16)


def local(
    dna_feats,
    conv_w,
    conv_gain,
    attn_gain,
    wq,
    wk,
    wv,
    wo,
    pair_w,
    pair_in,
    pair_gain,
    pair_w1,
    pair_w2,
):
    row_count = dna_feats.shape[0]
    reach = conv_w.shape[0] // 2
    rimmed = extended(dna_feats, ((("seq", "pr"), 0),), reach)
    channels = lax.all_gather(rimmed, "tp", axis=1, tiled=True)
    conv_empty = jnp.zeros((row_count, conv_w.shape[2]), jnp.float32)
    total = conv_empty
    piece = lax.all_gather(conv_w, "pr", axis=1, tiled=True)
    sliced = channels
    for offset in range(piece.shape[0]):
        total = total + jnp.dot(
            sliced[offset : offset + row_count], piece[offset], preferred_element_type=jnp.float32
        )
    squares = lax.psum(jnp.sum(total * total, axis=1, keepdims=True), "tp")
    model_width = total.shape[1] * lax.axis_size("tp")
    hidden_conv = jax.nn.gelu(
        total * lax.rsqrt(squares / model_width + EPSILON) * conv_gain
    ).astype(jnp.bfloat16)
    trunk_full = lax.all_gather(hidden_conv, "tp", axis=1, tiled=True)
    trunk_wide = trunk_full.astype(jnp.float32)
    normed = (trunk_wide * rms_scale(trunk_wide) * attn_gain).astype(jnp.bfloat16)
    query_width = wq.shape[1]
    pieces = (
        lax.all_gather(wq, "pr", axis=0, tiled=True),
        lax.all_gather(wk, "pr", axis=0, tiled=True),
        lax.all_gather(wv, "pr", axis=0, tiled=True),
    )
    sliced = normed
    query_sum, key_sum, value_sum = tuple(
        (jnp.dot(sliced, piece, preferred_element_type=jnp.float32) for piece in pieces)
    )
    head_count = query_width // QK
    queries = query_sum.astype(jnp.bfloat16).reshape(row_count, head_count, QK)
    keys_local = key_sum.astype(jnp.bfloat16).reshape(row_count, head_count, QK)
    values_local = value_sum.astype(jnp.bfloat16).reshape(row_count, head_count, HV)
    moved_query, moved_keys, moved_values = (
        lax.all_to_all(queries, "pr", split_axis=1, concat_axis=0, tiled=True),
        lax.all_to_all(keys_local, "pr", split_axis=1, concat_axis=0, tiled=True),
        lax.all_to_all(values_local, "pr", split_axis=1, concat_axis=0, tiled=True),
    )
    carried = attention_step(
        moved_query,
        attention_start(moved_query),
        (
            lax.all_gather(moved_keys, "seq", axis=0, tiled=True),
            lax.all_gather(moved_values, "seq", axis=0, tiled=True),
        ),
    )
    attended = lax.all_to_all(
        attention_finish(carried), "pr", split_axis=0, concat_axis=1, tiled=True
    )
    attended_flat = attended.reshape(row_count, head_count * HV)
    head_terms = jnp.dot(
        attended_flat,
        lax.all_gather(wo, "pr", axis=1, tiled=True),
        preferred_element_type=jnp.float32,
    )
    own_share = lax.psum_scatter(
        head_terms.astype(jnp.bfloat16), "tp", scatter_dimension=1, tiled=True
    ).astype(jnp.float32)
    trunk = (hidden_conv.astype(jnp.float32) + own_share).astype(jnp.bfloat16)
    pooled = trunk.astype(jnp.float32).reshape(row_count // POOL, POOL, -1).mean(axis=1)
    partial_embed = jnp.dot(pooled, pair_w.astype(jnp.float32), precision=lax.Precision.HIGHEST)
    embedded = lax.psum(partial_embed, "tp").astype(jnp.bfloat16)
    every_embed = lax.all_gather(embedded, ("seq", "pr"), axis=0, tiled=True)
    pair_rows = pair_in.shape[0]
    pair_cols = pair_in.shape[1]
    pair_width = pair_in.shape[2]
    row_first = lax.axis_index(("seq", "tp")) * pair_rows
    col_first = lax.axis_index("pr") * pair_cols
    row_embed = lax.dynamic_slice_in_dim(every_embed, row_first, pair_rows, 0)[
        :, :pair_width
    ].astype(jnp.float32)
    col_embed = lax.dynamic_slice_in_dim(every_embed, col_first, pair_cols, 0)[
        :, pair_width:
    ].astype(jnp.float32)
    summed = pair_in.astype(jnp.float32) + row_embed[:, None, :] + col_embed[None, :, :]
    pair_normed = (summed * rms_scale(summed) * pair_gain).astype(jnp.bfloat16)
    inner = jax.nn.gelu(
        jnp.dot(pair_normed.reshape(-1, pair_width), pair_w1, preferred_element_type=jnp.float32)
    ).astype(jnp.bfloat16)
    update = jnp.dot(inner, pair_w2, preferred_element_type=jnp.float32).reshape(summed.shape)
    pair_out = (summed + update).astype(jnp.bfloat16)
    return (trunk, pair_out)


def gelu_tanh(x):
    return 0.5 * x * (1.0 + jnp.tanh(math.sqrt(2.0 / math.pi) * (x + 0.044715 * (x * x * x))))


def to_rows(column):
    rows = column.shape[0]
    return jnp.transpose(jnp.broadcast_to(column, (rows, 128)))[:8]


def to_column(tile):
    rows = tile.shape[1]
    return jnp.transpose(jnp.broadcast_to(tile[:1], (128, rows)))[:, :1]


class Sems:
    def __init__(self, ref, limit):
        self.ref, self.limit, self.used = ref, limit, 0

    def take(self, count=1):
        first = self.used
        self.used += count
        assert self.used <= self.limit
        return first


def fold(ref, value):
    rows, extra = value.shape[0], value.shape[1] - 128
    ref[pl.ds(0, rows), :] = value[:, :128]
    depth = rows * extra // 128
    for i in range(128 // extra):
        ref[pl.ds(rows, depth), i * extra:(i + 1) * extra] = value[i * depth:(i + 1) * depth, 128:]


def unfold(ref, out):
    rows, extra = out.shape[0], out.shape[1] - 128
    out[:, :128] = ref[pl.ds(0, rows), :]
    depth = rows * extra // 128
    for i in range(128 // extra):
        out[pl.ds(i * depth, depth), 128:] = ref[pl.ds(rows, depth), i * extra:(i + 1) * extra]


SENDS = 96
RECVS = 96
HALO = 16


def fused_kernel(
    x_ref, cw_hbm, cg_ref, ag_ref, wq_hbm, wk_hbm, wv_hbm, wo_hbm, pw_hbm, pin_ref, pg_ref, w1_ref, w2_ref,
    trunk_ref, pout_ref,
    cw, wq, wk, wv, wo, pw,
    xin, xf, im, acc, accr, q1, q1r, hid, hall, s2, nrm, part, partr,
    qo, ko, vo, qb, kb, vb, ao, at, vf, af, ot, tin, eb, rowb, colb,
    lsem, ssem, rsem,
):
    s, t, p = lax.axis_index("seq"), lax.axis_index("tp"), lax.axis_index("pr")
    n_seq = lax.axis_size("seq")
    rows = x_ref.shape[0]
    cin = x_ref.shape[1]
    half = hid.shape[1]
    width = 2 * half
    sends, recvs = Sems(ssem, SENDS), Sems(rsem, RECVS)
    pending = []
    f32, bf16 = jnp.float32, jnp.bfloat16

    def remote(src, dst, recv, dev, cond=None):
        copy = pltpu.make_async_remote_copy(
            src_ref=src, dst_ref=dst, send_sem=ssem.at[sends.take()], recv_sem=rsem.at[recv],
            device_id=dev, device_id_type=pl.DeviceIdType.MESH,
        )
        if cond is None:
            copy.start()
        else:
            pl.when(cond)(lambda: copy.start())
        pending.append((copy, cond))

    def arrived(dst, recv, cond=None):
        copy = pltpu.make_async_remote_copy(
            src_ref=dst, dst_ref=dst, send_sem=ssem.at[0], recv_sem=rsem.at[recv],
            device_id={"pr": 1 - p}, device_id_type=pl.DeviceIdType.MESH,
        )
        if cond is None:
            copy.wait_recv()
        else:
            pl.when(cond)(lambda: copy.wait_recv())

    loads = [pltpu.make_async_copy(a, b, lsem.at[i]) for i, (a, b) in enumerate(
        ((cw_hbm, cw), (wq_hbm, wq), (wk_hbm, wk), (wv_hbm, wv), (wo_hbm, wo), (pw_hbm, pw)))]
    for load in loads:
        load.start()

    barrier = pltpu.get_barrier_semaphore()
    for ds in range(n_seq):
        for dt in range(2):
            for dp in range(2):
                if ds or dt or dp:
                    pl.semaphore_signal(
                        barrier, inc=1,
                        device_id={"seq": lax.rem(s + ds, n_seq), "tp": lax.rem(t + dt, 2), "pr": lax.rem(p + dp, 2)},
                        device_id_type=pl.DeviceIdType.MESH)
    pl.semaphore_wait(barrier, 4 * n_seq - 1)

    other_t, other_p = 1 - t, 1 - p
    diag = p == t
    off = p != t

    r_x = recvs.take(4)
    mine = pl.ds(pl.multiple_of(HALO + p * rows, HALO), rows)
    for td in (other_t, t):
        low, high = xin.at[pl.ds(0, HALO)], xin.at[pl.ds(HALO + 2 * rows, HALO)]
        remote(x_ref, xin.at[mine], r_x + p, {"tp": td, "pr": t}, None if td is other_t else off)
        remote(x_ref.at[pl.ds(rows - HALO, HALO)], low, r_x + 2,
               {"seq": lax.rem(s + 1, n_seq), "tp": td, "pr": t}, (p == 1) & (s < n_seq - 1))
        remote(x_ref.at[pl.ds(0, HALO)], high, r_x + 3,
               {"seq": lax.rem(s + n_seq - 1, n_seq), "tp": td, "pr": t}, (p == 0) & (s > 0))

    @pl.when(diag)
    def _():
        xin[mine, :] = x_ref[...]

    @pl.when(s == 0)
    def _():
        xin[pl.ds(0, HALO), :] = jnp.zeros((HALO, cin), bf16)

    @pl.when(s == n_seq - 1)
    def _():
        xin[pl.ds(HALO + 2 * rows, HALO), :] = jnp.zeros((HALO, cin), bf16)

    for q in range(2):
        arrived(xin.at[pl.ds(HALO + q * rows, rows)], r_x + q, off | (p != q))
    arrived(xin.at[pl.ds(0, HALO)], r_x + 2, s > 0)
    arrived(xin.at[pl.ds(HALO + 2 * rows, HALO)], r_x + 3, s < n_seq - 1)

    xf[...] = xin[...].astype(f32)
    taps = im.shape[1] // cin
    for o in range(taps):
        im[:, o * cin:(o + 1) * cin] = xf[pl.ds(HALO - taps // 2 + o, 2 * rows), :].astype(bf16)

    own = pl.ds(pl.multiple_of(p * rows, rows), rows)
    theirs = pl.ds(pl.multiple_of(other_p * rows, rows), rows)
    partner = {"pr": other_p}
    loads[0].wait()
    step = 256
    chunks = half // step
    r_c = recvs.take(chunks)
    for c in range(chunks):
        cols = pl.ds(c * step, step)
        acc[:, cols] = jnp.dot(im[...], cw[:, cols], preferred_element_type=f32)
        remote(acc.at[theirs, cols], accr.at[:, cols], r_c + c, partner)
    square = jnp.zeros((rows, 1), f32)
    for c in range(chunks):
        cols = pl.ds(c * step, step)
        arrived(accr.at[:, cols], r_c + c)
        value = acc[own, cols] + accr[:, cols]
        accr[:, cols] = value
        square = square + jnp.sum(value * value, axis=1, keepdims=True)
    q1[...] = to_rows(square)
    r_q = recvs.take()
    remote(q1, q1r, r_q, {"tp": other_t})
    arrived(q1r, r_q)
    scale = to_column(lax.rsqrt((q1[...] + q1r[...]) / width + EPSILON))

    me4 = t * 2 + p
    r_h = recvs.take(2 * chunks)
    hmine = own
    square = jnp.zeros((rows, 1), f32)
    for c in range(chunks):
        cols = pl.ds(c * step, step)
        rounded = gelu_tanh(accr[:, cols] * scale * cg_ref[cols][None, :]).astype(bf16)
        hid[:, cols] = rounded
        wide = rounded.astype(f32)
        square = square + jnp.sum(wide * wide, axis=1, keepdims=True)
        remote(hid.at[:, cols], hall.at[hmine, cols], r_h + 2 * c + p, {"tp": other_t, "pr": t})
        remote(hid.at[:, cols], hall.at[hmine, cols], r_h + 2 * c + p, {"pr": t}, off)
    s2[me4] = to_rows(square)
    r_s = recvs.take(4)
    for dt in range(2):
        for dp in range(2):
            if dt or dp:
                remote(s2.at[me4], s2.at[me4], r_s + me4, {"tp": lax.rem(t + dt, 2), "pr": lax.rem(p + dp, 2)})

    @pl.when(diag)
    def _():
        hall[hmine, :] = hid[...]

    gain = jnp.where(p == 0, ag_ref[pl.ds(0, half)][None, :], ag_ref[pl.ds(half, half)][None, :])
    for i in range(4):
        arrived(s2.at[i], r_s + i, me4 != i)
    for q in range(2):
        for c in range(chunks):
            arrived(hall.at[pl.ds(q * rows, rows), pl.ds(c * step, step)], r_h + 2 * c + q, off | (p != q))
        scale = to_column(lax.rsqrt((s2[q] + s2[2 + q]) / width + EPSILON))
        block = pl.ds(q * rows, rows)
        nrm[block, :] = (hall[block, :].astype(f32) * scale * gain).astype(bf16)

    for load in loads[1:]:
        load.wait()
    heads = n_seq
    qk = heads * QK
    base_k, base_v, base_q = 0, qk, qk + heads * HV
    plan = [(wk, base_k, c) for c in range(qk // step)] + [
        (wv, base_v, c) for c in range(heads * HV // step)] + [(wq, base_q, c) for c in range(qk // step)]
    r_p = recvs.take(len(plan))
    def multiply(i):
        w, base, c = plan[i]
        cols = pl.ds(base + c * step, step)
        part[:, cols] = jnp.dot(nrm[...], w[:, c * step:(c + 1) * step], preferred_element_type=f32)
        remote(part.at[theirs, cols], partr.at[:, cols], r_p + i, partner)

    def finish(i):
        w, base, c = plan[i]
        cols = pl.ds(base + c * step, step)
        arrived(partr.at[:, cols], r_p + i)

    def total(first, count):
        return (part[own, first:first + count] + partr[:, first:first + count]).astype(bf16)

    far = (2, 1, 3) if n_seq == 4 else tuple(range(1, n_seq))

    def scatter(src, dst_of, recv):
        for d in far:
            h = lax.rem(s + d, n_seq)
            remote(src.at[h], dst_of(s), recv + d, {"seq": h})

    r_k, r_v, r_qq = recvs.take(n_seq), recvs.take(n_seq), recvs.take(n_seq)
    n_k, n_v = qk // step, heads * HV // step
    last_k, last_v = n_k, n_k + n_v
    for i in range(last_k + 1):
        multiply(i)
    for i in range(last_k):
        finish(i)
    for h in range(heads):
        ko[h] = total(base_k + h * QK, QK)
    scatter(ko, lambda j: kb.at[j, p], r_k)
    kb[s, p] = ko[s]
    for i in range(last_k + 1, last_v + 1):
        multiply(i)
    for i in range(last_k, last_v):
        finish(i)
    for h in range(heads):
        fold(vo.at[h], total(base_v + h * HV, HV))
    scatter(vo, lambda j: vb.at[j, p], r_v)
    vb[s, p] = vo[s]
    for i in range(last_v + 1, len(plan)):
        multiply(i)
    for i in range(last_v, len(plan)):
        finish(i)
    for h in range(heads):
        qo[h] = total(base_q + h * QK, QK)
    scatter(qo, lambda j: qb.at[j], r_qq)
    qb[s] = qo[s]

    r_k2, r_v2 = recvs.take(n_seq), recvs.take(n_seq)
    near = (0, 1, 3, 2) if n_seq == 4 else tuple(range(n_seq))
    for buf, got, on in ((kb, r_k, r_k2), (vb, r_v, r_v2)):
        for d in near:
            j = lax.rem(s + n_seq - d, n_seq)
            if d:
                arrived(buf.at[j, p], got + d)
            remote(buf.at[j, p], buf.at[j, p], on + d, partner)
    for buf, on in ((kb, r_k2), (vb, r_v2)):
        for d in near:
            j = lax.rem(s + n_seq - d, n_seq)
            arrived(buf.at[j, other_p], on + d)

    factor = 1.0 / math.sqrt(QK)
    r_a, r_a2 = recvs.take(n_seq), recvs.take(n_seq)
    keys_total = 2 * n_seq * rows
    for j in range(n_seq):
        for q in range(2):
            unfold(vb.at[j, q], vf.at[j, q])
    turns = far + (0,)
    for first in range(0, n_seq, 2):
        pair_of = turns[first:first + 2]
        blocks = [lax.rem(s + n_seq - d, n_seq) for d in pair_of]
        for d, j in zip(pair_of, blocks):
            if d:
                arrived(qb.at[j], r_qq + d)
        scores = lax.dot_general(
            jnp.concatenate([qb[j] for j in blocks], axis=0), kb[...].reshape(keys_total, QK),
            (((1,), (1,)), ((), ())), preferred_element_type=f32) * factor
        weights = jnp.exp(scores - jnp.max(scores, axis=1, keepdims=True))
        sums = jnp.sum(weights, axis=1, keepdims=True)
        mixed = jnp.dot(weights.astype(bf16), vf[...].reshape(keys_total, HV), preferred_element_type=f32)
        result = (mixed / sums).astype(bf16)
        for i, (d, j) in enumerate(zip(pair_of, blocks)):
            piece = result[i * rows:(i + 1) * rows]
            if d:
                fold(ao.at[d], piece)
                remote(ao.at[d], at.at[s, p], r_a + d, {"seq": j})
            else:
                fold(at.at[s, p], piece)
    for d in (0,) + far[::-1]:
        h = lax.rem(s + d, n_seq)
        if d:
            arrived(at.at[h, p], r_a + d)
        remote(at.at[h, p], at.at[h, p], r_a2 + d, partner)
    for d in range(n_seq):
        arrived(at.at[lax.rem(s + d, n_seq), other_p], r_a2 + d)

    for h in range(heads):
        for q in range(2):
            unfold(at.at[h, q], af.at[h, q])
    r_o = recvs.take(2 * chunks)
    for c in range(chunks):
        cols = pl.ds(c * step, step)
        value = jnp.zeros((2 * rows, step), f32)
        for h in range(heads):
            value = value + jnp.dot(
                af[h].reshape(2 * rows, HV), wo[h * HV:(h + 1) * HV, cols], preferred_element_type=f32)
        ot[:, cols] = value.astype(bf16)
        remote(ot.at[theirs, cols], tin.at[t, :, cols], r_o + 2 * c + t, {"tp": p, "pr": other_p})
        remote(ot.at[own, cols], tin.at[t, :, cols], r_o + 2 * c + t, {"tp": p}, off)

        @pl.when(diag)
        def _():
            tin[t, :, cols] = ot[own, cols]

    partial = jnp.zeros((8, 2 * pin_ref.shape[2]), f32)
    groups = rows // POOL
    for c in range(chunks):
        cols = pl.ds(c * step, step)
        for i in range(2):
            arrived(tin.at[i, :, cols], r_o + 2 * c + i, off | (t != i))
        trunk = (hid[:, cols].astype(f32) + (tin[0, :, cols].astype(f32) + tin[1, :, cols].astype(f32))).astype(bf16)
        trunk_ref[:, cols] = trunk
        pooled = jnp.sum(trunk.astype(f32).reshape(groups, POOL, step), axis=1) * (1.0 / POOL)
        first = pooled.astype(bf16)
        rest = pooled - first.astype(f32)
        second = rest.astype(bf16)
        third = (rest - second.astype(f32)).astype(bf16)
        for piece in (third, second, first):
            partial = partial + jnp.dot(piece, pw[c * step:(c + 1) * step, :], preferred_element_type=f32)
    pair = pin_ref.shape[2]
    eb[0] = partial[:, :pair]
    eb[1] = partial[:, pair:]
    r_r, r_e = recvs.take(2), recvs.take(8)
    remote(eb.at[0], rowb.at[t], r_r + t, {"tp": p, "pr": other_p})
    remote(eb.at[0], rowb.at[t], r_r + t, {"tp": p}, off)

    @pl.when(diag)
    def _():
        rowb[t] = eb[0]

    side = s // 2
    slot = lax.rem(s, 2) * 2 + p
    for d in far + (0,):
        for dt in range(2):
            remote(eb.at[1], colb.at[t, slot], r_e + t * 4 + slot,
                   {"seq": lax.rem(s + d, n_seq), "tp": lax.rem(t + dt, 2), "pr": side},
                   (p != side) if d == 0 and dt == 0 else None)

    @pl.when(p == side)
    def _():
        colb[t, slot] = eb[1]

    for i in range(2):
        arrived(rowb.at[i], r_r + i, off | (t != i))
    for i in range(2):
        for k in range(4):
            arrived(colb.at[i, k], r_e + i * 4 + k, (t != i) | (slot != k) | (p != side))
    row_embed = (rowb[0] + rowb[1]).astype(bf16).astype(f32)
    col_embed = (colb[0] + colb[1]).reshape(4 * groups, pair).astype(bf16).astype(f32)
    summed = pin_ref[...].astype(f32) + row_embed[:, None, :] + col_embed[None, :, :]
    flat = summed.reshape(-1, pair)
    inv = lax.rsqrt(jnp.mean(flat * flat, axis=1, keepdims=True) + EPSILON)
    normal = (flat * inv * pg_ref[...]).astype(bf16)
    inner = gelu_tanh(jnp.dot(normal, w1_ref[...], preferred_element_type=f32)).astype(bf16)
    update = jnp.dot(inner, w2_ref[...], preferred_element_type=f32)
    pout_ref[...] = (flat + update).astype(bf16).reshape(pout_ref.shape)

    for copy, cond in pending:
        if cond is None:
            copy.wait_send()
        else:
            pl.when(cond)(lambda copy=copy: copy.wait_send())


def fused(dna_feats, conv_w, conv_gain, attn_gain, wq, wk, wv, wo, pair_w, pair_in, pair_gain, pair_w1, pair_w2):
    rows, cin = dna_feats.shape
    taps, _, half = conv_w.shape
    heads = lax.axis_size("seq")
    width = half * 2
    bf16, f32 = jnp.bfloat16, jnp.float32
    vmem = pl.BlockSpec(memory_space=pltpu.VMEM)
    hbm = pl.BlockSpec(memory_space=pltpu.HBM)
    flat_conv = conv_w.reshape(taps * cin, half)
    total = heads * (2 * QK + HV)
    pair = pair_in.shape[2]
    groups = rows // POOL
    packed = rows * HV // 128
    v = pltpu.VMEM
    scratch = [
        v(flat_conv.shape, bf16), v(wq.shape, bf16), v(wk.shape, bf16), v(wv.shape, bf16), v(wo.shape, bf16),
        v(pair_w.shape, bf16),
        v((2 * rows + 2 * HALO, cin), bf16), v((2 * rows + 2 * HALO, cin), f32), v((2 * rows, taps * cin), bf16),
        v((2 * rows, half), f32), v((rows, half), f32), v((8, rows), f32), v((8, rows), f32),
        v((rows, half), bf16), v((2 * rows, half), bf16), v((4, 8, rows), f32), v((2 * rows, half), bf16),
        v((2 * rows, total), f32), v((rows, total), f32),
        v((heads, rows, QK), bf16), v((heads, rows, QK), bf16), v((heads, packed, 128), bf16),
        v((heads, rows, QK), bf16), v((heads, 2, rows, QK), bf16), v((heads, 2, packed, 128), bf16),
        v((heads, packed, 128), bf16), v((heads, 2, packed, 128), bf16),
        v((heads, 2, rows, HV), bf16), v((heads, 2, rows, HV), bf16),
        v((2 * rows, half), bf16), v((2, rows, half), bf16),
        v((2, groups, pair), f32), v((2, groups, pair), f32), v((2, 4, groups, pair), f32),
        pltpu.SemaphoreType.DMA((8,)), pltpu.SemaphoreType.DMA((SENDS,)), pltpu.SemaphoreType.DMA((RECVS,)),
    ]
    return pl.pallas_call(
        fused_kernel,
        out_shape=(jax.ShapeDtypeStruct((rows, half), bf16), jax.ShapeDtypeStruct(pair_in.shape, bf16)),
        in_specs=[vmem, hbm, vmem, vmem, hbm, hbm, hbm, hbm, hbm, vmem, vmem, vmem, vmem],
        out_specs=(vmem, vmem),
        scratch_shapes=scratch,
        compiler_params=pltpu.CompilerParams(
            collective_id=0, has_side_effects=True, vmem_limit_bytes=60 * 1024 * 1024),
    )(dna_feats, flat_conv, conv_gain, attn_gain, wq, wk, wv, wo, pair_w,
      pair_in, pair_gain.reshape(1, pair), pair_w1, pair_w2)


def block(*arrays):
    dna_feats, conv_w, wq = arrays[0], arrays[1], arrays[4]
    n_seq, n_tp, n_pr = (lax.axis_size(a) for a in ("seq", "tp", "pr"))
    fits = (
        n_tp == 2 and n_pr == 2 and n_seq == 4 and wq.shape[1] == n_seq * QK
        and dna_feats.shape[0] == 128 and conv_w.shape[1] == dna_feats.shape[1]
        and arrays[3].shape[0] == 2 * conv_w.shape[2] and conv_w.shape[2] % 256 == 0
        and arrays[9].shape[0] * POOL == dna_feats.shape[0]
    )
    return fused(*arrays) if fits else local(*arrays)


def solution(mesh):
    in_specs = (
        P(("grp", "seq", "pr"), "tp"),
        P(None, "pr", "tp"),
        P("tp"),
        P(),
        P("pr", "tp"),
        P("pr", "tp"),
        P("pr", "tp"),
        P("tp", "pr"),
        P("tp", None),
        P(("grp", "seq", "tp"), "pr", None),
        P(),
        P(),
        P(),
    )
    out_specs = (P(("grp", "seq", "pr"), "tp"), P(("grp", "seq", "tp"), "pr", None))
    return jax.shard_map(block, mesh=mesh, in_specs=in_specs, out_specs=out_specs, check_vma=False)
```

```python
import math

import jax
import jax.numpy as jnp
from jax import lax
from jax.experimental import pallas as pl
from jax.experimental.pallas import tpu as pltpu
from jax.sharding import PartitionSpec as P

QK = 128
HV = 192
POOL = 16


EPSILON = 1e-06


def extended(value, sides, width):
    for axis, dim in sides:
        devices, length = (lax.axis_size(axis), value.shape[dim])
        up = [(i, (i + 1) % devices) for i in range(devices - 1)]
        down = [(j, i) for i, j in up]
        last = lax.slice_in_dim(value, length - width, length, axis=dim)
        first = lax.slice_in_dim(value, 0, width, axis=dim)
        before = lax.ppermute(last, axis, up)
        after = lax.ppermute(first, axis, down)
        value = jnp.concatenate([before, value, after], axis=dim)
    return value


def rms_scale(values):
    return lax.rsqrt(jnp.mean(values * values, axis=-1, keepdims=True) + EPSILON)


def attention_start(query_block):
    head_count = query_block.shape[1]
    row_count = query_block.shape[0]
    highest = jnp.full((head_count, row_count), -1e30, jnp.float32)
    totals = jnp.zeros((head_count, row_count), jnp.float32)
    mixed = jnp.zeros((row_count, head_count, HV), jnp.float32)
    return (highest, totals, mixed)


def attention_step(query_block, carry, pieces):
    factor = 1.0 / math.sqrt(QK)
    highest, totals, mixed = carry
    key_piece, value_piece = pieces
    scores = (
        jnp.einsum("qhd,khd->hqk", query_block, key_piece, preferred_element_type=jnp.float32)
        * factor
    )
    new_high = jnp.maximum(highest, jnp.max(scores, axis=-1))
    weights = jnp.exp(scores - new_high[:, :, None])
    totals = jnp.sum(weights, axis=-1)
    added = jnp.einsum(
        "hqk,khd->qhd",
        weights.astype(jnp.bfloat16),
        value_piece,
        preferred_element_type=jnp.float32,
    )
    mixed = added
    return (new_high, totals, mixed)


def attention_finish(carry):
    highest, totals, mixed = carry
    return (mixed / jnp.transpose(totals)[:, :, None]).astype(jnp.bfloat16)


def local(
    dna_feats,
    conv_w,
    conv_gain,
    attn_gain,
    wq,
    wk,
    wv,
    wo,
    pair_w,
    pair_in,
    pair_gain,
    pair_w1,
    pair_w2,
):
    row_count = dna_feats.shape[0]
    reach = conv_w.shape[0] // 2
    rimmed = extended(dna_feats, ((("seq", "pr"), 0),), reach)
    channels = lax.all_gather(rimmed, "tp", axis=1, tiled=True)
    conv_empty = jnp.zeros((row_count, conv_w.shape[2]), jnp.float32)
    total = conv_empty
    piece = lax.all_gather(conv_w, "pr", axis=1, tiled=True)
    sliced = channels
    for offset in range(piece.shape[0]):
        total = total + jnp.dot(
            sliced[offset : offset + row_count], piece[offset], preferred_element_type=jnp.float32
        )
    squares = lax.psum(jnp.sum(total * total, axis=1, keepdims=True), "tp")
    model_width = total.shape[1] * lax.axis_size("tp")
    hidden_conv = jax.nn.gelu(
        total * lax.rsqrt(squares / model_width + EPSILON) * conv_gain
    ).astype(jnp.bfloat16)
    trunk_full = lax.all_gather(hidden_conv, "tp", axis=1, tiled=True)
    trunk_wide = trunk_full.astype(jnp.float32)
    normed = (trunk_wide * rms_scale(trunk_wide) * attn_gain).astype(jnp.bfloat16)
    query_width = wq.shape[1]
    pieces = (
        lax.all_gather(wq, "pr", axis=0, tiled=True),
        lax.all_gather(wk, "pr", axis=0, tiled=True),
        lax.all_gather(wv, "pr", axis=0, tiled=True),
    )
    sliced = normed
    query_sum, key_sum, value_sum = tuple(
        (jnp.dot(sliced, piece, preferred_element_type=jnp.float32) for piece in pieces)
    )
    head_count = query_width // QK
    queries = query_sum.astype(jnp.bfloat16).reshape(row_count, head_count, QK)
    keys_local = key_sum.astype(jnp.bfloat16).reshape(row_count, head_count, QK)
    values_local = value_sum.astype(jnp.bfloat16).reshape(row_count, head_count, HV)
    moved_query, moved_keys, moved_values = (
        lax.all_to_all(queries, "pr", split_axis=1, concat_axis=0, tiled=True),
        lax.all_to_all(keys_local, "pr", split_axis=1, concat_axis=0, tiled=True),
        lax.all_to_all(values_local, "pr", split_axis=1, concat_axis=0, tiled=True),
    )
    carried = attention_step(
        moved_query,
        attention_start(moved_query),
        (
            lax.all_gather(moved_keys, "seq", axis=0, tiled=True),
            lax.all_gather(moved_values, "seq", axis=0, tiled=True),
        ),
    )
    attended = lax.all_to_all(
        attention_finish(carried), "pr", split_axis=0, concat_axis=1, tiled=True
    )
    attended_flat = attended.reshape(row_count, head_count * HV)
    head_terms = jnp.dot(
        attended_flat,
        lax.all_gather(wo, "pr", axis=1, tiled=True),
        preferred_element_type=jnp.float32,
    )
    own_share = lax.psum_scatter(
        head_terms.astype(jnp.bfloat16), "tp", scatter_dimension=1, tiled=True
    ).astype(jnp.float32)
    trunk = (hidden_conv.astype(jnp.float32) + own_share).astype(jnp.bfloat16)
    pooled = trunk.astype(jnp.float32).reshape(row_count // POOL, POOL, -1).mean(axis=1)
    partial_embed = jnp.dot(pooled, pair_w.astype(jnp.float32), precision=lax.Precision.HIGHEST)
    embedded = lax.psum(partial_embed, "tp").astype(jnp.bfloat16)
    every_embed = lax.all_gather(embedded, ("seq", "pr"), axis=0, tiled=True)
    pair_rows = pair_in.shape[0]
    pair_cols = pair_in.shape[1]
    pair_width = pair_in.shape[2]
    row_first = lax.axis_index(("seq", "tp")) * pair_rows
    col_first = lax.axis_index("pr") * pair_cols
    row_embed = lax.dynamic_slice_in_dim(every_embed, row_first, pair_rows, 0)[
        :, :pair_width
    ].astype(jnp.float32)
    col_embed = lax.dynamic_slice_in_dim(every_embed, col_first, pair_cols, 0)[
        :, pair_width:
    ].astype(jnp.float32)
    summed = pair_in.astype(jnp.float32) + row_embed[:, None, :] + col_embed[None, :, :]
    pair_normed = (summed * rms_scale(summed) * pair_gain).astype(jnp.bfloat16)
    inner = jax.nn.gelu(
        jnp.dot(pair_normed.reshape(-1, pair_width), pair_w1, preferred_element_type=jnp.float32)
    ).astype(jnp.bfloat16)
    update = jnp.dot(inner, pair_w2, preferred_element_type=jnp.float32).reshape(summed.shape)
    pair_out = (summed + update).astype(jnp.bfloat16)
    return (trunk, pair_out)


def gelu_tanh(x):
    return 0.5 * x * (1.0 + jnp.tanh(math.sqrt(2.0 / math.pi) * (x + 0.044715 * (x * x * x))))


def to_rows(column):
    rows = column.shape[0]
    return jnp.transpose(jnp.broadcast_to(column, (rows, 128)))[:8]


def to_column(tile):
    rows = tile.shape[1]
    return jnp.transpose(jnp.broadcast_to(tile[:1], (128, rows)))[:, :1]


class Sems:
    def __init__(self, ref, limit):
        self.ref, self.limit, self.used = ref, limit, 0

    def take(self, count=1):
        first = self.used
        self.used += count
        assert self.used <= self.limit
        return first


def fold(ref, value):
    rows, extra = value.shape[0], value.shape[1] - 128
    ref[pl.ds(0, rows), :] = value[:, :128]
    depth = rows * extra // 128
    for i in range(128 // extra):
        ref[pl.ds(rows, depth), i * extra:(i + 1) * extra] = value[i * depth:(i + 1) * depth, 128:]


def unfold(ref, out):
    rows, extra = out.shape[0], out.shape[1] - 128
    out[:, :128] = ref[pl.ds(0, rows), :]
    depth = rows * extra // 128
    for i in range(128 // extra):
        out[pl.ds(i * depth, depth), 128:] = ref[pl.ds(rows, depth), i * extra:(i + 1) * extra]


SENDS = 96
RECVS = 96
HALO = 16


def fused_kernel(
    x_ref, cw_hbm, cg_ref, ag_ref, wq_hbm, wk_hbm, wv_hbm, wo_hbm, pw_hbm, pin_ref, pg_ref, w1_ref, w2_ref,
    trunk_ref, pout_ref,
    cw, wq, wk, wv, wo, pw,
    xin, xf, im, acc, accr, q1, q1r, hid, hall, s2, nrm, part, partr,
    qo, ko, vo, qb, kb, vb, ao, at, vf, af, ws, ot, tin, eb, rowb, colb,
    lsem, ssem, rsem,
):
    s, t, p = lax.axis_index("seq"), lax.axis_index("tp"), lax.axis_index("pr")
    n_seq = lax.axis_size("seq")
    rows = x_ref.shape[0]
    cin = x_ref.shape[1]
    half = hid.shape[1]
    width = 2 * half
    sends, recvs = Sems(ssem, SENDS), Sems(rsem, RECVS)
    pending = []
    f32, bf16 = jnp.float32, jnp.bfloat16

    def remote(src, dst, recv, dev, cond=None):
        copy = pltpu.make_async_remote_copy(
            src_ref=src, dst_ref=dst, send_sem=ssem.at[sends.take()], recv_sem=rsem.at[recv],
            device_id=dev, device_id_type=pl.DeviceIdType.MESH,
        )
        if cond is None:
            copy.start()
        else:
            pl.when(cond)(lambda: copy.start())
        pending.append((copy, cond))

    def arrived(dst, recv, cond=None):
        copy = pltpu.make_async_remote_copy(
            src_ref=dst, dst_ref=dst, send_sem=ssem.at[0], recv_sem=rsem.at[recv],
            device_id={"pr": 1 - p}, device_id_type=pl.DeviceIdType.MESH,
        )
        if cond is None:
            copy.wait_recv()
        else:
            pl.when(cond)(lambda: copy.wait_recv())

    loads = [pltpu.make_async_copy(a, b, lsem.at[i]) for i, (a, b) in enumerate(
        ((cw_hbm, cw), (wq_hbm, wq), (wk_hbm, wk), (wv_hbm, wv), (wo_hbm, wo), (pw_hbm, pw)))]
    for load in loads:
        load.start()

    barrier = pltpu.get_barrier_semaphore()
    for ds in range(n_seq):
        for dt in range(2):
            for dp in range(2):
                if ds or dt or dp:
                    pl.semaphore_signal(
                        barrier, inc=1,
                        device_id={"seq": lax.rem(s + ds, n_seq), "tp": lax.rem(t + dt, 2), "pr": lax.rem(p + dp, 2)},
                        device_id_type=pl.DeviceIdType.MESH)
    pl.semaphore_wait(barrier, 4 * n_seq - 1)

    other_t, other_p = 1 - t, 1 - p
    diag = p == t
    off = p != t

    r_x = recvs.take(4)
    mine = pl.ds(pl.multiple_of(HALO + p * rows, HALO), rows)
    for td in (other_t, t):
        low, high = xin.at[pl.ds(0, HALO)], xin.at[pl.ds(HALO + 2 * rows, HALO)]
        remote(x_ref, xin.at[mine], r_x + p, {"tp": td, "pr": t}, None if td is other_t else off)
        remote(x_ref.at[pl.ds(rows - HALO, HALO)], low, r_x + 2,
               {"seq": lax.rem(s + 1, n_seq), "tp": td, "pr": t}, (p == 1) & (s < n_seq - 1))
        remote(x_ref.at[pl.ds(0, HALO)], high, r_x + 3,
               {"seq": lax.rem(s + n_seq - 1, n_seq), "tp": td, "pr": t}, (p == 0) & (s > 0))

    @pl.when(diag)
    def _():
        xin[mine, :] = x_ref[...]

    @pl.when(s == 0)
    def _():
        xin[pl.ds(0, HALO), :] = jnp.zeros((HALO, cin), bf16)

    @pl.when(s == n_seq - 1)
    def _():
        xin[pl.ds(HALO + 2 * rows, HALO), :] = jnp.zeros((HALO, cin), bf16)

    for q in range(2):
        arrived(xin.at[pl.ds(HALO + q * rows, rows)], r_x + q, off | (p != q))
    arrived(xin.at[pl.ds(0, HALO)], r_x + 2, s > 0)
    arrived(xin.at[pl.ds(HALO + 2 * rows, HALO)], r_x + 3, s < n_seq - 1)

    xf[...] = xin[...].astype(f32)
    taps = im.shape[1] // cin
    for o in range(taps):
        im[:, o * cin:(o + 1) * cin] = xf[pl.ds(HALO - taps // 2 + o, 2 * rows), :].astype(bf16)

    own = pl.ds(pl.multiple_of(p * rows, rows), rows)
    theirs = pl.ds(pl.multiple_of(other_p * rows, rows), rows)
    partner = {"pr": other_p}
    loads[0].wait()
    step = 256
    chunks = half // step
    r_c = recvs.take(chunks)
    for c in range(chunks):
        cols = pl.ds(c * step, step)
        acc[:, cols] = jnp.dot(im[...], cw[:, cols], preferred_element_type=f32)
        remote(acc.at[theirs, cols], accr.at[:, cols], r_c + c, partner)
    square = jnp.zeros((rows, 1), f32)
    for c in range(chunks):
        cols = pl.ds(c * step, step)
        arrived(accr.at[:, cols], r_c + c)
        value = acc[own, cols] + accr[:, cols]
        accr[:, cols] = value
        square = square + jnp.sum(value * value, axis=1, keepdims=True)
    q1[...] = to_rows(square)
    r_q = recvs.take()
    remote(q1, q1r, r_q, {"tp": other_t})
    arrived(q1r, r_q)
    scale = to_column(lax.rsqrt((q1[...] + q1r[...]) / width + EPSILON))

    me4 = t * 2 + p
    r_h = recvs.take(2 * chunks)
    hmine = own
    square = jnp.zeros((rows, 1), f32)
    for c in range(chunks):
        cols = pl.ds(c * step, step)
        rounded = gelu_tanh(accr[:, cols] * scale * cg_ref[cols][None, :]).astype(bf16)
        hid[:, cols] = rounded
        wide = rounded.astype(f32)
        square = square + jnp.sum(wide * wide, axis=1, keepdims=True)
        remote(hid.at[:, cols], hall.at[hmine, cols], r_h + 2 * c + p, {"tp": other_t, "pr": t})
        remote(hid.at[:, cols], hall.at[hmine, cols], r_h + 2 * c + p, {"pr": t}, off)
    s2[me4] = to_rows(square)
    r_s = recvs.take(4)
    for dt in range(2):
        for dp in range(2):
            if dt or dp:
                remote(s2.at[me4], s2.at[me4], r_s + me4, {"tp": lax.rem(t + dt, 2), "pr": lax.rem(p + dp, 2)})

    @pl.when(diag)
    def _():
        hall[hmine, :] = hid[...]

    gain = jnp.where(p == 0, ag_ref[pl.ds(0, half)][None, :], ag_ref[pl.ds(half, half)][None, :])
    for i in range(4):
        arrived(s2.at[i], r_s + i, me4 != i)
    for q in range(2):
        for c in range(chunks):
            arrived(hall.at[pl.ds(q * rows, rows), pl.ds(c * step, step)], r_h + 2 * c + q, off | (p != q))
        scale = to_column(lax.rsqrt((s2[q] + s2[2 + q]) / width + EPSILON))
        block = pl.ds(q * rows, rows)
        nrm[block, :] = (hall[block, :].astype(f32) * scale * gain).astype(bf16)

    for load in loads[1:]:
        load.wait()
    heads = n_seq
    qk = heads * QK
    base_k, base_v, base_q = 0, qk, qk + heads * HV
    plan = [(wk, base_k, c) for c in range(qk // step)] + [
        (wq, base_q, c) for c in range(qk // step)] + [(wv, base_v, c) for c in range(heads * HV // step)]
    r_p = recvs.take(len(plan))
    def multiply(i):
        w, base, c = plan[i]
        cols = pl.ds(base + c * step, step)
        part[:, cols] = jnp.dot(nrm[...], w[:, c * step:(c + 1) * step], preferred_element_type=f32)
        remote(part.at[theirs, cols], partr.at[:, cols], r_p + i, partner)

    def finish(i):
        w, base, c = plan[i]
        cols = pl.ds(base + c * step, step)
        arrived(partr.at[:, cols], r_p + i)

    def total(first, count):
        return (part[own, first:first + count] + partr[:, first:first + count]).astype(bf16)

    far = (2, 1, 3) if n_seq == 4 else tuple(range(1, n_seq))

    def scatter(src, dst_of, recv):
        for d in far:
            h = lax.rem(s + d, n_seq)
            remote(src.at[h], dst_of(s), recv + d, {"seq": h})

    r_k, r_v, r_qq = recvs.take(n_seq), recvs.take(n_seq), recvs.take(n_seq)
    last_k, last_q = qk // step, 2 * qk // step
    for i in range(last_k + 1):
        multiply(i)
    for i in range(last_k):
        finish(i)
    for h in range(heads):
        ko[h] = total(base_k + h * QK, QK)
    scatter(ko, lambda j: kb.at[j, p], r_k)
    kb[s, p] = ko[s]
    for i in range(last_k + 1, last_q + 1):
        multiply(i)
    for i in range(last_k, last_q):
        finish(i)
    for h in range(heads):
        qo[h] = total(base_q + h * QK, QK)
    scatter(qo, lambda j: qb.at[j], r_qq)
    qb[s] = qo[s]
    for i in range(last_q + 1, len(plan)):
        multiply(i)
    for i in range(last_q, len(plan)):
        finish(i)
    for h in range(heads):
        fold(vo.at[h], total(base_v + h * HV, HV))
    scatter(vo, lambda j: vb.at[j, p], r_v)
    vb[s, p] = vo[s]

    r_k2, r_v2 = recvs.take(n_seq), recvs.take(n_seq)
    near = (0, 1, 3, 2) if n_seq == 4 else tuple(range(n_seq))
    for d in near:
        j = lax.rem(s + n_seq - d, n_seq)
        if d:
            arrived(kb.at[j, p], r_k + d)
        remote(kb.at[j, p], kb.at[j, p], r_k2 + d, partner)
    for d in near:
        arrived(kb.at[lax.rem(s + n_seq - d, n_seq), other_p], r_k2 + d)

    factor = 1.0 / math.sqrt(QK)
    r_a, r_a2 = recvs.take(n_seq), recvs.take(n_seq)
    keys_total = 2 * n_seq * rows
    turns = far + (0,)
    scored = []
    for first in range(0, n_seq, 2):
        pair_of = turns[first:first + 2]
        blocks = [lax.rem(s + n_seq - d, n_seq) for d in pair_of]
        for d, j in zip(pair_of, blocks):
            if d:
                arrived(qb.at[j], r_qq + d)
        scores = lax.dot_general(
            jnp.concatenate([qb[j] for j in blocks], axis=0), kb[...].reshape(keys_total, QK),
            (((1,), (1,)), ((), ())), preferred_element_type=f32) * factor
        weights = jnp.exp(scores - jnp.max(scores, axis=1, keepdims=True))
        ws[first // 2] = weights.astype(bf16)
        scored.append((pair_of, blocks, jnp.sum(weights, axis=1, keepdims=True)))
    for d in near:
        j = lax.rem(s + n_seq - d, n_seq)
        if d:
            arrived(vb.at[j, p], r_v + d)
        remote(vb.at[j, p], vb.at[j, p], r_v2 + d, partner)
        unfold(vb.at[j, p], vf.at[j, p])
    for d in near:
        j = lax.rem(s + n_seq - d, n_seq)
        arrived(vb.at[j, other_p], r_v2 + d)
        unfold(vb.at[j, other_p], vf.at[j, other_p])
    for index, (pair_of, blocks, sums) in enumerate(scored):
        mixed = jnp.dot(ws[index], vf[...].reshape(keys_total, HV), preferred_element_type=f32)
        result = (mixed / sums).astype(bf16)
        for i, (d, j) in enumerate(zip(pair_of, blocks)):
            piece = result[i * rows:(i + 1) * rows]
            if d:
                fold(ao.at[d], piece)
                remote(ao.at[d], at.at[s, p], r_a + d, {"seq": j})
            else:
                fold(at.at[s, p], piece)
    for d in (0,) + far[::-1]:
        h = lax.rem(s + d, n_seq)
        if d:
            arrived(at.at[h, p], r_a + d)
        remote(at.at[h, p], at.at[h, p], r_a2 + d, partner)
    for d in range(n_seq):
        arrived(at.at[lax.rem(s + d, n_seq), other_p], r_a2 + d)

    for h in range(heads):
        for q in range(2):
            unfold(at.at[h, q], af.at[h, q])
    r_o = recvs.take(2 * chunks)
    for c in range(chunks):
        cols = pl.ds(c * step, step)
        value = jnp.zeros((2 * rows, step), f32)
        for h in range(heads):
            value = value + jnp.dot(
                af[h].reshape(2 * rows, HV), wo[h * HV:(h + 1) * HV, cols], preferred_element_type=f32)
        ot[:, cols] = value.astype(bf16)
        remote(ot.at[theirs, cols], tin.at[t, :, cols], r_o + 2 * c + t, {"tp": p, "pr": other_p})
        remote(ot.at[own, cols], tin.at[t, :, cols], r_o + 2 * c + t, {"tp": p}, off)

        @pl.when(diag)
        def _():
            tin[t, :, cols] = ot[own, cols]

    partial = jnp.zeros((8, 2 * pin_ref.shape[2]), f32)
    groups = rows // POOL
    for c in range(chunks):
        cols = pl.ds(c * step, step)
        for i in range(2):
            arrived(tin.at[i, :, cols], r_o + 2 * c + i, off | (t != i))
        trunk = (hid[:, cols].astype(f32) + (tin[0, :, cols].astype(f32) + tin[1, :, cols].astype(f32))).astype(bf16)
        trunk_ref[:, cols] = trunk
        pooled = jnp.sum(trunk.astype(f32).reshape(groups, POOL, step), axis=1) * (1.0 / POOL)
        first = pooled.astype(bf16)
        rest = pooled - first.astype(f32)
        second = rest.astype(bf16)
        third = (rest - second.astype(f32)).astype(bf16)
        for piece in (third, second, first):
            partial = partial + jnp.dot(piece, pw[c * step:(c + 1) * step, :], preferred_element_type=f32)
    pair = pin_ref.shape[2]
    eb[0] = partial[:, :pair]
    eb[1] = partial[:, pair:]
    r_r, r_e = recvs.take(2), recvs.take(8)
    remote(eb.at[0], rowb.at[t], r_r + t, {"tp": p, "pr": other_p})
    remote(eb.at[0], rowb.at[t], r_r + t, {"tp": p}, off)

    @pl.when(diag)
    def _():
        rowb[t] = eb[0]

    side = s // 2
    slot = lax.rem(s, 2) * 2 + p
    for d in far + (0,):
        for dt in range(2):
            remote(eb.at[1], colb.at[t, slot], r_e + t * 4 + slot,
                   {"seq": lax.rem(s + d, n_seq), "tp": lax.rem(t + dt, 2), "pr": side},
                   (p != side) if d == 0 and dt == 0 else None)

    @pl.when(p == side)
    def _():
        colb[t, slot] = eb[1]

    for i in range(2):
        arrived(rowb.at[i], r_r + i, off | (t != i))
    for i in range(2):
        for k in range(4):
            arrived(colb.at[i, k], r_e + i * 4 + k, (t != i) | (slot != k) | (p != side))
    row_embed = (rowb[0] + rowb[1]).astype(bf16).astype(f32)
    col_embed = (colb[0] + colb[1]).reshape(4 * groups, pair).astype(bf16).astype(f32)
    summed = pin_ref[...].astype(f32) + row_embed[:, None, :] + col_embed[None, :, :]
    flat = summed.reshape(-1, pair)
    inv = lax.rsqrt(jnp.mean(flat * flat, axis=1, keepdims=True) + EPSILON)
    normal = (flat * inv * pg_ref[...]).astype(bf16)
    inner = gelu_tanh(jnp.dot(normal, w1_ref[...], preferred_element_type=f32)).astype(bf16)
    update = jnp.dot(inner, w2_ref[...], preferred_element_type=f32)
    pout_ref[...] = (flat + update).astype(bf16).reshape(pout_ref.shape)

    for copy, cond in pending:
        if cond is None:
            copy.wait_send()
        else:
            pl.when(cond)(lambda copy=copy: copy.wait_send())


def fused(dna_feats, conv_w, conv_gain, attn_gain, wq, wk, wv, wo, pair_w, pair_in, pair_gain, pair_w1, pair_w2):
    rows, cin = dna_feats.shape
    taps, _, half = conv_w.shape
    heads = lax.axis_size("seq")
    width = half * 2
    bf16, f32 = jnp.bfloat16, jnp.float32
    vmem = pl.BlockSpec(memory_space=pltpu.VMEM)
    hbm = pl.BlockSpec(memory_space=pltpu.HBM)
    flat_conv = conv_w.reshape(taps * cin, half)
    total = heads * (2 * QK + HV)
    pair = pair_in.shape[2]
    groups = rows // POOL
    packed = rows * HV // 128
    v = pltpu.VMEM
    scratch = [
        v(flat_conv.shape, bf16), v(wq.shape, bf16), v(wk.shape, bf16), v(wv.shape, bf16), v(wo.shape, bf16),
        v(pair_w.shape, bf16),
        v((2 * rows + 2 * HALO, cin), bf16), v((2 * rows + 2 * HALO, cin), f32), v((2 * rows, taps * cin), bf16),
        v((2 * rows, half), f32), v((rows, half), f32), v((8, rows), f32), v((8, rows), f32),
        v((rows, half), bf16), v((2 * rows, half), bf16), v((4, 8, rows), f32), v((2 * rows, half), bf16),
        v((2 * rows, total), f32), v((rows, total), f32),
        v((heads, rows, QK), bf16), v((heads, rows, QK), bf16), v((heads, packed, 128), bf16),
        v((heads, rows, QK), bf16), v((heads, 2, rows, QK), bf16), v((heads, 2, packed, 128), bf16),
        v((heads, packed, 128), bf16), v((heads, 2, packed, 128), bf16),
        v((heads, 2, rows, HV), bf16), v((heads, 2, rows, HV), bf16),
        v((heads // 2, 2 * rows, 2 * heads * rows), bf16),
        v((2 * rows, half), bf16), v((2, rows, half), bf16),
        v((2, groups, pair), f32), v((2, groups, pair), f32), v((2, 4, groups, pair), f32),
        pltpu.SemaphoreType.DMA((8,)), pltpu.SemaphoreType.DMA((SENDS,)), pltpu.SemaphoreType.DMA((RECVS,)),
    ]
    return pl.pallas_call(
        fused_kernel,
        out_shape=(v((rows, half), bf16), v(pair_in.shape, bf16)),
        in_specs=[vmem, hbm, vmem, vmem, hbm, hbm, hbm, hbm, hbm, vmem, vmem, vmem, vmem],
        out_specs=(vmem, vmem),
        scratch_shapes=scratch,
        compiler_params=pltpu.CompilerParams(
            collective_id=0, has_side_effects=True, vmem_limit_bytes=60 * 1024 * 1024),
    )(dna_feats, flat_conv, conv_gain, attn_gain, wq, wk, wv, wo, pair_w,
      pair_in, pair_gain.reshape(1, pair), pair_w1, pair_w2)


def block(*arrays):
    dna_feats, conv_w, wq = arrays[0], arrays[1], arrays[4]
    n_seq, n_tp, n_pr = (lax.axis_size(a) for a in ("seq", "tp", "pr"))
    fits = (
        n_tp == 2 and n_pr == 2 and n_seq == 4 and wq.shape[1] == n_seq * QK
        and dna_feats.shape[0] == 128 and conv_w.shape[1] == dna_feats.shape[1]
        and arrays[3].shape[0] == 2 * conv_w.shape[2] and conv_w.shape[2] % 256 == 0
        and arrays[9].shape[0] * POOL == dna_feats.shape[0]
    )
    return fused(*arrays) if fits else local(*arrays)


def solution(mesh):
    in_specs = (
        P(("grp", "seq", "pr"), "tp"),
        P(None, "pr", "tp"),
        P("tp"),
        P(),
        P("pr", "tp"),
        P("pr", "tp"),
        P("pr", "tp"),
        P("tp", "pr"),
        P("tp", None),
        P(("grp", "seq", "tp"), "pr", None),
        P(),
        P(),
        P(),
    )
    out_specs = (P(("grp", "seq", "pr"), "tp"), P(("grp", "seq", "tp"), "pr", None))
    return jax.shard_map(block, mesh=mesh, in_specs=in_specs, out_specs=out_specs, check_vma=False)
```
